512 devices in a mesh: section: 4 (over x_hi, core), head: 16 (over y, x_lo), kv: 8 (over z).
Axes of the slice: x: 4 (x_hi: 2, x_lo: 2; x = x_hi * 2 + x_lo), y: 8, z: 8, core: 2. Of those that a mesh axis runs over, the one named last changes fastest.
Arguments:
- tokens: bfloat16 [4, 1024, 4096], P('section', 'kv', 'head'), may hold values from -40 to 40
- w_query: bfloat16 [4096, 4096], P(('section', 'kv'), 'head'), may hold values from -0.21875 to 0.21875
- w_keyvalue: bfloat16 [4096, 2, 4096], P(('section', 'kv'), None, 'head'), may hold values from -0.09375 to 0.09375
- cache_keys: bfloat16 [4, 16384, 4096], P('section', 'kv', 'head'), may hold values from -800 to 800
- cache_values: bfloat16 [4, 16384, 4096], P('section', 'kv', 'head'), may hold values from -6 to 6
- key_start: int32 [4], P('section'), may hold values from 0 to 8191
- key_end: int32 [4], P('section'), may hold values from 12288 to 16384
- w_out: bfloat16 [4096, 4096], P('head', ('section', 'kv')), may hold values from -0.375 to 0.375
Outputs:
- attention_out: bfloat16 [4, 1024, 4096], P('section', 'kv', 'head')
The draws below stay inside these ranges and needn't reach their ends.
All inputs are finite; a program needn't handle non-finite values.
Results may differ from the reference program's by a relative error of at most 0.014.
The reference program's roundings to bfloat16 on the way (of `normed`, `queries`, `weights` and `attended`) count: a program that leaves them out, or rounds other values in their place, can miss the bound.
Values may be sent and summed in bfloat16 or wider, within the bound.
No kernel may reach another device: no remote copies, remote signals or barrier semaphores. Data moves between devices by JAX's collectives and lax.ppermute only.
A program may use at most 64 MiB of HBM per device.

```python
import jax
import jax.numpy as jnp
from jax import lax

D = 4096
H = 32
HD = 128
SAMPLES = 4
NEW = 1024
CTX = 16384


def draw_tokens(key, part):
    base_key, column_key, row_key = jax.random.split(jax.random.fold_in(key, 11), 3)
    column_scale = jnp.exp(jax.random.uniform(column_key, (1, 1, D), jnp.float32, -1.15, 1.15))
    row_scale = jnp.exp(jax.random.uniform(row_key, (SAMPLES, NEW, 1), jnp.float32, -0.8, 0.8))
    base_draw = jax.random.normal(base_key, (SAMPLES, NEW, D), jnp.float32)
    return jnp.clip(base_draw * column_scale * row_scale, -40.0, 40.0).astype(jnp.bfloat16)


def draw_cache_keys(key, part):
    base_key = jax.random.fold_in(jax.random.fold_in(key, 23), 0)
    base_draw = jax.random.normal(base_key, (SAMPLES, CTX, D), jnp.float32)
    return jnp.clip(base_draw, -6.0, 6.0).astype(jnp.bfloat16)


def with_ends(entries, rng, least, high):
    place = [jax.random.randint(jax.random.fold_in(rng, axis), (), 0, length) for axis, length in enumerate(entries.shape)]
    widest = entries.shape.index(max(entries.shape))
    beside = place[:widest] + [(place[widest] + 1) % entries.shape[widest]] + place[widest + 1:]
    return entries.at[tuple(place)].set(least).at[tuple(beside)].set(high)


def level_of(stream_key, shape, cuts, smallest, high):
    level, own = 1.0, jax.random.fold_in(stream_key, 6)
    for dim, blocks in cuts:
        steps = jnp.exp(jax.random.uniform(jax.random.fold_in(own, dim), (blocks,), jnp.float32, smallest / len(cuts), high / len(cuts)))
        level = level * jnp.repeat(steps, shape[dim] // blocks).reshape([-1 if axis == dim else 1 for axis in range(len(shape))])
    return level


def bell_draw(stream_key, extent, width, most, cuts=(), kind=jnp.bfloat16):
    level = level_of(stream_key, extent, cuts, -0.22, 0.18) if cuts else 1.0
    entries = jax.random.normal(stream_key, extent, jnp.float32) * width * level
    return jnp.minimum(jnp.maximum(entries, -most), most).astype(kind)


def setup_inputs(seed: int = 0) -> dict:
    splits = jax.random.split(jax.random.key(seed), 9)
    return {
        "tokens": draw_tokens(jax.random.fold_in(splits[8], 71), 0),
        "w_query": bell_draw(splits[1], (D, D), (D // 5) ** -0.5, 0.21875, ((0, 32), (1, 16))),
        "w_keyvalue": bell_draw(splits[2], (D, 2, D), D ** -0.5, 0.09375, ((0, 32), (2, 16))),
        "cache_keys": draw_cache_keys(jax.random.fold_in(splits[8], 71), 0),
        "cache_values": bell_draw(splits[4], (SAMPLES, CTX, D), 1.0, 6.0, ((0, 4), (1, 8), (2, 16))),
        "key_start": with_ends(jax.random.randint(splits[5], (SAMPLES,), 0, CTX // 2), jax.random.fold_in(splits[5], 1), 0, (CTX // 2) - 1).astype(jnp.int32),
        "key_end": with_ends(jax.random.randint(splits[6], (SAMPLES,), 3 * CTX // 4, CTX + 1), jax.random.fold_in(splits[6], 1), 3 * CTX // 4, CTX).astype(jnp.int32),
        "w_out": bell_draw(splits[7], (D, D), (D // 16) ** -0.5, 0.375, ((0, 16), (1, 32))),
    }


def reference(tokens, w_query, w_keyvalue, cache_keys, cache_values, key_start, key_end, w_out):
    widened = tokens.astype(jnp.float32)
    scaled = widened * lax.rsqrt(lax.optimization_barrier(jnp.mean(widened * widened, axis=2, keepdims=True)) + 1e-05)
    normed = scaled.astype(jnp.bfloat16).reshape(SAMPLES * NEW, D)
    queries = jnp.dot(normed, w_query, preferred_element_type=jnp.float32).astype(jnp.bfloat16)
    pair_sums = jnp.dot(normed, w_keyvalue.reshape(D, 2 * D), preferred_element_type=jnp.float32).astype(jnp.bfloat16)
    queries = queries.reshape(SAMPLES, NEW, H, HD)
    new_keys = pair_sums[:, :D].reshape(SAMPLES, NEW, H, HD)
    new_values = pair_sums[:, D:].reshape(SAMPLES, NEW, H, HD)
    keys_all = jnp.concatenate([cache_keys.reshape(SAMPLES, CTX, H, HD), new_keys], axis=1)
    values_all = jnp.concatenate([cache_values.reshape(SAMPLES, CTX, H, HD), new_values], axis=1)
    key_place = jnp.arange(CTX + NEW, dtype=jnp.int32)
    row_place = jnp.arange(NEW, dtype=jnp.int32)
    score_scale = HD ** (-0.5)

    def one_sample(packed):
        query_sample, keys_sample, values_sample, window_begin, window_stop = packed
        cache_usable = (key_place < CTX) & (key_place >= window_begin) & (key_place < window_stop)
        new_usable = (key_place[None, :] >= CTX) & (key_place[None, :] - CTX <= row_place[:, None])
        usable = cache_usable[None, :] | new_usable

        def one_head(head_pack):
            query_head, keys_head, values_head = head_pack
            scores = jnp.dot(query_head, keys_head.T, preferred_element_type=jnp.float32) * score_scale
            masked = jnp.where(usable, scores, -1e+30)
            row_peak = lax.optimization_barrier(jnp.max(masked, axis=1, keepdims=True))
            weights = jnp.where(usable, jnp.exp(masked - row_peak), 0.0).astype(jnp.bfloat16)
            row_total = lax.optimization_barrier(jnp.sum(weights.astype(jnp.float32), axis=1, keepdims=True))
            mixture = jnp.dot(weights, values_head, preferred_element_type=jnp.float32)
            return mixture / row_total
        heads_out = lax.map(one_head, (query_sample.transpose(1, 0, 2), keys_sample.transpose(1, 0, 2), values_sample.transpose(1, 0, 2)))
        return heads_out.transpose(1, 0, 2).reshape(NEW, D)
    attended = lax.map(one_sample, (queries, keys_all, values_all, key_start, key_end))
    attended = attended.astype(jnp.bfloat16).reshape(SAMPLES * NEW, D)
    projected = jnp.dot(attended, w_out, preferred_element_type=jnp.float32).astype(jnp.bfloat16)
    return projected.reshape(SAMPLES, NEW, D)
```

```python
import jax
import jax.numpy as jnp
from jax import lax
from jax.experimental import pallas as pl
from jax.experimental.pallas import tpu as pltpu
from jax.sharding import Mesh
from jax.sharding import PartitionSpec as P

HD = 128
HEAD = ("y", "x_lo")
ROWS = ("x_hi", "kv")
STAT_ROWS = 16
QUERY_ROWS = 512
KEY_ROWS = 512
DEAD = -1e30
SCALE = HD**-0.5
EXPONENT = SCALE * 1.4426950408889634
VMEM = pltpu.CompilerParams(vmem_limit_bytes=48 * 1024 * 1024)
SCALAR = pl.BlockSpec(memory_space=pltpu.SMEM)
WHOLE = pl.BlockSpec(memory_space=pltpu.VMEM)


def dot(a, b):
    return jnp.dot(a, b, preferred_element_type=jnp.float32)


def shared(value, axes):
    copies = jnp.broadcast_to(value, (lax.axis_size(axes), *value.shape))
    return lax.all_to_all(copies, axes, split_axis=0, concat_axis=0, tiled=True)


def swapped(value):
    return lax.ppermute(value, "core", [(0, 1), (1, 0)])


def normalize_kernel(core_ref, x_ref, keep_ref, send_ref):
    core = core_ref[0]
    blocks = x_ref.shape[0]
    squares = None
    for b in range(blocks):
        x = x_ref[b].astype(jnp.float32)
        squares = x * x if squares is None else squares + x * x
    mean = jnp.sum(squares, axis=1, keepdims=True) / (blocks * x_ref.shape[2])
    factor = lax.rsqrt(mean + 1e-05)
    for half in range(2):
        for j in range(4):
            for out_ref, side in ((keep_ref, core), (send_ref, 1 - core)):
                x = x_ref[half * 8 + side * 4 + j].astype(jnp.float32)
                out_ref[half * 4 + j] = (x * factor).astype(jnp.bfloat16)


def project_kernel(own_ref, other_ref, w_ref, own_out, other_out):
    rows = own_ref.shape[1]
    total = None
    for b in range(own_ref.shape[0]):
        x = jnp.concatenate([own_ref[b], other_ref[b]], axis=0)
        part = dot(x, w_ref[b])
        total = part if total is None else total + part
    own_out[...] = total[:rows]
    other_out[...] = total[rows:]


def thirds(value):
    high = value.astype(jnp.bfloat16)
    rest = value - high.astype(jnp.float32)
    middle = rest.astype(jnp.bfloat16)
    low = (rest - middle.astype(jnp.float32)).astype(jnp.bfloat16)
    return [high.astype(jnp.float32), middle.astype(jnp.float32), low.astype(jnp.float32)]


def attend_kernel(kv_ref, bias_ref, q_ref, k_ref, v_ref, new_k_ref, new_v_ref, out_ref, s_ref):
    first = pl.program_id(1) * QUERY_ROWS
    q = q_ref[...]
    cache_rows = k_ref.shape[0]
    new_rows = new_k_ref.shape[0]

    def score(keys):
        return lax.dot_general(q, keys, (((1,), (1,)), ((), ())), preferred_element_type=jnp.float32)

    peak = None
    for at in range(0, cache_rows, KEY_ROWS):
        s = score(k_ref[at : at + KEY_ROWS]) + bias_ref[0:1, at : at + KEY_ROWS]
        s_ref[:, at : at + KEY_ROWS] = s
        for lane in range(0, KEY_ROWS, HD):
            piece = s[:, lane : lane + HD]
            peak = piece if peak is None else jnp.maximum(peak, piece)
    s = score(new_k_ref[...])
    row = first + lax.broadcasted_iota(jnp.int32, s.shape, 0)
    column = kv_ref[0] * new_rows + lax.broadcasted_iota(jnp.int32, s.shape, 1)
    s = jnp.where(column <= row, s, DEAD)
    s_ref[:, cache_rows:] = s
    peak = jnp.max(jnp.maximum(peak, s), axis=1, keepdims=True)

    def mixed(at, values):
        weights = jnp.exp2((s_ref[:, at : at + values.shape[0]] - peak) * EXPONENT)
        both = jnp.concatenate([values, jnp.ones_like(values)], axis=1)
        return dot(weights.astype(jnp.bfloat16), both)

    total = mixed(cache_rows, new_v_ref[...])
    for at in range(0, cache_rows, KEY_ROWS):
        total = total + mixed(at, v_ref[at : at + KEY_ROWS])

    lane = lax.broadcasted_iota(jnp.int32, (HD, HD), 1)
    blocks, rows, _ = out_ref.shape
    own = rows - STAT_ROWS
    for b in range(blocks):
        part = total[b * own : (b + 1) * own]
        out_ref[b, :own] = part[:, :HD].astype(jnp.bfloat16)
        turned = jnp.where(lane == 0, peak[b * own : (b + 1) * own], part[:, HD:]).T
        stats = thirds(turned[0:1]) + thirds(turned[1:2])
        stats = jnp.concatenate([*stats, jnp.zeros((STAT_ROWS - 6, HD), jnp.float32)], axis=0)
        out_ref[b, own:] = stats.astype(jnp.bfloat16)


def finish_kernel(core_ref, parts_ref, own_w_ref, other_w_ref, out_ref):
    core = core_ref[0]
    sources, rows, width = parts_ref.shape
    own = rows - STAT_ROWS
    heads = []
    for at in range(0, width, HD):
        stats = [parts_ref[z, own:, at : at + HD].astype(jnp.float32) for z in range(sources)]
        peaks = [s[0:1] + s[1:2] + s[2:3] for s in stats]
        totals = [s[3:4] + s[4:5] + s[5:6] for s in stats]
        highest = peaks[0]
        for p in peaks[1:]:
            highest = jnp.maximum(highest, p)
        factors = [jnp.exp2((p - highest) * EXPONENT) for p in peaks]
        total = sum(f * t for f, t in zip(factors, totals))
        shares = [f / total for f in factors]
        shares = jnp.concatenate([*shares, jnp.zeros((HD - sources, HD), jnp.float32)], axis=0).T
        mixture = None
        for z in range(sources):
            part = parts_ref[z, :own, at : at + HD].astype(jnp.float32) * shares[:, z : z + 1]
            mixture = part if mixture is None else mixture + part
        heads.append(mixture.astype(jnp.bfloat16))
    attended = jnp.concatenate(heads, axis=1)
    half = own_w_ref.shape[0] // 2
    for x_hi in range(2):
        for pair in range(half // 2):
            for w_ref, side in ((own_w_ref, core), (other_w_ref, 1 - core)):
                at = x_hi * half + pair * 2
                w = jnp.concatenate([w_ref[at], w_ref[at + 1]], axis=1)
                out_ref[x_hi * half + side * (half // 2) + pair] = dot(attended, w).astype(jnp.bfloat16)


def shards(tokens, w_query, w_keyvalue, cache_keys, cache_values, key_start, key_end, w_out):
    local_rows, width = tokens.shape[1:]
    cache_rows = cache_keys.shape[1]
    core = lax.axis_index("core").astype(jnp.int32).reshape(1)
    kv = lax.axis_index("kv").astype(jnp.int32)
    kv_count = lax.axis_size("kv")

    gathered = shared(tokens[0], HEAD)
    query_w = shared(w_query, ROWS).reshape(8, 256, width)
    pair_w = shared(w_keyvalue.reshape(-1, 2 * width), ROWS).reshape(8, 256, 2 * width)
    out_w = shared(w_out, ROWS)
    out_w_other = swapped(out_w)

    half_shape = jax.ShapeDtypeStruct((8, local_rows, width), jnp.bfloat16)
    keep, send = pl.pallas_call(
        normalize_kernel,
        out_shape=(half_shape, half_shape),
        in_specs=[SCALAR, WHOLE],
        out_specs=(WHOLE, WHOLE),
        compiler_params=VMEM,
        name="normalize",
    )(core, gathered)
    other = swapped(send)

    def project(w, name):
        shape = jax.ShapeDtypeStruct((local_rows, w.shape[2]), jnp.float32)
        mine, theirs = pl.pallas_call(
            project_kernel,
            out_shape=(shape, shape),
            in_specs=[WHOLE] * 3,
            out_specs=(WHOLE, WHOLE),
            compiler_params=VMEM,
            name=name,
        )(keep, other, w)
        return (mine + swapped(theirs)).astype(jnp.bfloat16)

    queries = shared(project(query_w, "project_queries"), "kv").reshape(-1, width)
    pair = project(pair_w, "project_pair")
    place = kv * cache_rows + lax.iota(jnp.int32, cache_rows)
    usable = (place >= key_start[0]) & (place < key_end[0])
    bias = jnp.broadcast_to(jnp.where(usable, 0.0, DEAD).astype(jnp.float32)[None], (8, cache_rows))

    blocks = QUERY_ROWS // local_rows
    padded = local_rows + STAT_ROWS
    parts = pl.pallas_call(
        attend_kernel,
        grid=(width // HD, queries.shape[0] // QUERY_ROWS),
        out_shape=jax.ShapeDtypeStruct((kv_count, padded, width), jnp.bfloat16),
        in_specs=[
            SCALAR,
            pl.BlockSpec((8, cache_rows), lambda h, i: (0, 0)),
            pl.BlockSpec((QUERY_ROWS, HD), lambda h, i: (i, h)),
            pl.BlockSpec((cache_rows, HD), lambda h, i: (0, h)),
            pl.BlockSpec((cache_rows, HD), lambda h, i: (0, h)),
            pl.BlockSpec((local_rows, HD), lambda h, i: (0, h)),
            pl.BlockSpec((local_rows, HD), lambda h, i: (0, h + width // HD)),
        ],
        out_specs=pl.BlockSpec((blocks, padded, HD), lambda h, i: (i, 0, h)),
        scratch_shapes=[pltpu.VMEM((QUERY_ROWS, cache_rows + local_rows), jnp.float32)],
        compiler_params=VMEM,
        name="attend",
    )(kv.reshape(1), bias, queries, cache_keys[0], cache_values[0], pair, pair)

    arrived = lax.all_to_all(parts, "kv", split_axis=0, concat_axis=0, tiled=True)
    columns = pl.pallas_call(
        finish_kernel,
        out_shape=jax.ShapeDtypeStruct((lax.axis_size(HEAD), local_rows, width), jnp.bfloat16),
        in_specs=[SCALAR, WHOLE, WHOLE, WHOLE],
        out_specs=WHOLE,
        compiler_params=VMEM,
        name="finish",
    )(core, arrived, out_w, out_w_other)
    columns = lax.all_to_all(columns, HEAD, split_axis=0, concat_axis=0, tiled=True)
    return columns.astype(jnp.float32).sum(axis=0).astype(jnp.bfloat16)[None]


def solution(mesh):
    section, head, kv = (mesh.shape[name] for name in ("section", "head", "kv"))
    torus = Mesh(
        mesh.devices.reshape(section // 2, 2, head // 2, 2, kv),
        ("x_hi", "core", "y", "x_lo", "kv"),
    )
    section = ("x_hi", "core")
    rows = ("x_hi", "core", "kv")
    return jax.shard_map(
        shards,
        mesh=torus,
        in_specs=(
            P(section, "kv", HEAD),
            P(rows, HEAD),
            P(rows, None, HEAD),
            P(section, "kv", HEAD),
            P(section, "kv", HEAD),
            P(section),
            P(section),
            P(HEAD, rows),
        ),
        out_specs=P(section, "kv", HEAD),
        check_vma=False,
    )
```

```python
import jax
import jax.numpy as jnp
from jax import lax
from jax.experimental import pallas as pl
from jax.experimental.pallas import tpu as pltpu
from jax.sharding import Mesh
from jax.sharding import PartitionSpec as P

HD = 128
HEAD = ("y", "x_lo")
KV = ("z_4", "z_2", "z_1")
STAT_ROWS = 16
QUERY_ROWS = 512
KEY_ROWS = 512
DEAD = -1e30
SCALE = HD**-0.5
EXPONENT = SCALE * 1.4426950408889634
VMEM = pltpu.CompilerParams(vmem_limit_bytes=48 * 1024 * 1024)
SCALAR = pl.BlockSpec(memory_space=pltpu.SMEM)
WHOLE = pl.BlockSpec(memory_space=pltpu.VMEM)


def dot(a, b):
    return jnp.dot(a, b, preferred_element_type=jnp.float32)


def shared(value, axes):
    copies = jnp.broadcast_to(value, (lax.axis_size(axes), *value.shape))
    return lax.all_to_all(copies, axes, split_axis=0, concat_axis=0, tiled=True)


def swapped(value, axis):
    return lax.ppermute(value, axis, [(0, 1), (1, 0)])


def normalize_kernel(place_ref, x_ref, keep_ref, send_ref):
    x_hi, core = place_ref[0], place_ref[1]
    blocks = x_ref.shape[0]
    squares = None
    for b in range(blocks):
        x = x_ref[b].astype(jnp.float32)
        squares = x * x if squares is None else squares + x * x
    mean = jnp.sum(squares, axis=1, keepdims=True) / (blocks * x_ref.shape[2])
    factor = lax.rsqrt(mean + 1e-05)
    for far in range(2):
        half = 1 - x_hi if far else x_hi
        for j in range(4):
            for out_ref, side in ((keep_ref, core), (send_ref, 1 - core)):
                x = x_ref[half * 8 + side * 4 + j].astype(jnp.float32)
                out_ref[far, j] = (x * factor).astype(jnp.bfloat16)


def project(place_ref, tiles, w_ref, far_w_ref, order):
    kv = place_ref[2]
    lanes = w_ref.shape[1]
    near = pl.multiple_of((kv & 1) * lanes, lanes)
    away = pl.multiple_of((1 - (kv & 1)) * lanes, lanes)
    total = None
    for at in range(w_ref.shape[0]):
        rows = order(at, kv)
        for ref, lane in ((w_ref, near), (far_w_ref, away)):
            x = jnp.concatenate([tile(rows, pl.ds(lane, lanes)) for tile in tiles], axis=0)
            part = dot(x, ref[at])
            total = part if total is None else total + part
    return total


def query_kernel(place_ref, keep_ref, other_ref, w_ref, far_w_ref, own_out, other_out):
    def order(at, kv):
        far, flip_4, flip_2 = at % 2, at // 2 % 2, at // 4
        return far, (kv >> 1) ^ (2 * flip_4 + flip_2)

    def tile(ref):
        return lambda rows, lanes: ref[rows[0], rows[1], :, lanes]

    total = project(place_ref, [tile(keep_ref), tile(other_ref)], w_ref, far_w_ref, order)
    own_out[...] = total[: own_out.shape[0]]
    other_out[...] = total[own_out.shape[0] :]


def pair_kernel(place_ref, keep_ref, other_ref, far_ref, w_ref, far_w_ref, own_out, other_out):
    def order(at, kv):
        flip_4, flip_2 = at % 2, at // 2
        return (kv >> 1) ^ (2 * flip_4 + flip_2)

    def tile(ref, side):
        return lambda rows, lanes: ref[side, rows, :, lanes]

    tiles = [tile(keep_ref, 0), tile(far_ref, 0), tile(other_ref, 0), tile(far_ref, 1)]
    total = project(place_ref, tiles, w_ref, far_w_ref, order)
    rows = own_out.shape[1]
    for n in range(2):
        own_out[n] = total[n * rows : (n + 1) * rows]
        other_out[n] = total[(n + 2) * rows : (n + 3) * rows]


def thirds(value):
    high = value.astype(jnp.bfloat16)
    rest = value - high.astype(jnp.float32)
    middle = rest.astype(jnp.bfloat16)
    low = (rest - middle.astype(jnp.float32)).astype(jnp.bfloat16)
    return [high.astype(jnp.float32), middle.astype(jnp.float32), low.astype(jnp.float32)]


def attend_kernel(kv_ref, bias_ref, q_ref, k_ref, v_ref, new_k_ref, new_v_ref, out_ref, s_ref):
    first = pl.program_id(1) * QUERY_ROWS
    q = q_ref[...]
    cache_rows = k_ref.shape[0]
    new_rows = new_k_ref.shape[0]

    def score(keys):
        return lax.dot_general(q, keys, (((1,), (1,)), ((), ())), preferred_element_type=jnp.float32)

    peak = None
    for at in range(0, cache_rows, KEY_ROWS):
        s = score(k_ref[at : at + KEY_ROWS]) + bias_ref[0:1, at : at + KEY_ROWS]
        s_ref[:, at : at + KEY_ROWS] = s
        for lane in range(0, KEY_ROWS, HD):
            piece = s[:, lane : lane + HD]
            peak = piece if peak is None else jnp.maximum(peak, piece)
    s = score(new_k_ref[...])
    row = first + lax.broadcasted_iota(jnp.int32, s.shape, 0)
    column = kv_ref[0] * new_rows + lax.broadcasted_iota(jnp.int32, s.shape, 1)
    s = jnp.where(column <= row, s, DEAD)
    s_ref[:, cache_rows:] = s
    peak = jnp.max(jnp.maximum(peak, s), axis=1, keepdims=True)

    def mixed(at, values):
        weights = jnp.exp2((s_ref[:, at : at + values.shape[0]] - peak) * EXPONENT)
        both = jnp.concatenate([values, jnp.ones_like(values)], axis=1)
        return dot(weights.astype(jnp.bfloat16), both)

    total = mixed(cache_rows, new_v_ref[...])
    for at in range(0, cache_rows, KEY_ROWS):
        total = total + mixed(at, v_ref[at : at + KEY_ROWS])

    lane = lax.broadcasted_iota(jnp.int32, (HD, HD), 1)
    blocks, rows, _ = out_ref.shape
    own = rows - STAT_ROWS
    for b in range(blocks):
        part = total[b * own : (b + 1) * own]
        out_ref[b, :own] = part[:, :HD].astype(jnp.bfloat16)
        turned = jnp.where(lane == 0, peak[b * own : (b + 1) * own], part[:, HD:]).T
        stats = thirds(turned[0:1]) + thirds(turned[1:2])
        stats = jnp.concatenate([*stats, jnp.zeros((STAT_ROWS - 6, HD), jnp.float32)], axis=0)
        out_ref[b, own:] = stats.astype(jnp.bfloat16)


def finish_kernel(place_ref, parts_ref, w_ref, far_w_ref, swap_w_ref, swap_far_w_ref, out_ref):
    x_hi, core, kv = place_ref[0], place_ref[1], place_ref[2]
    sources, rows, width = parts_ref.shape
    own = rows - STAT_ROWS
    heads = []
    for at in range(0, width, HD):
        stats = [parts_ref[z, own:, at : at + HD].astype(jnp.float32) for z in range(sources)]
        peaks = [s[0:1] + s[1:2] + s[2:3] for s in stats]
        totals = [s[3:4] + s[4:5] + s[5:6] for s in stats]
        highest = peaks[0]
        for p in peaks[1:]:
            highest = jnp.maximum(highest, p)
        factors = [jnp.exp2((p - highest) * EXPONENT) for p in peaks]
        total = sum(f * t for f, t in zip(factors, totals))
        shares = [f / total for f in factors]
        shares = jnp.concatenate([*shares, jnp.zeros((HD - sources, HD), jnp.float32)], axis=0).T
        mixture = None
        for z in range(sources):
            part = parts_ref[z, :own, at : at + HD].astype(jnp.float32) * shares[:, z : z + 1]
            mixture = part if mixture is None else mixture + part
        heads.append(mixture.astype(jnp.bfloat16))
    attended = jnp.concatenate(heads, axis=1)
    lanes = w_ref.shape[2]
    near = pl.multiple_of((kv & 1) * lanes, lanes)
    away = pl.multiple_of((1 - (kv & 1)) * lanes, lanes)
    for at in range(w_ref.shape[0]):
        far, flip_4, flip_2 = at % 2, at // 2 % 2, at // 4
        section = 2 * (x_hi ^ far)
        pair = (kv >> 1) ^ (2 * flip_4 + flip_2)
        for near_ref, away_ref, side in ((w_ref, far_w_ref, core), (swap_w_ref, swap_far_w_ref, 1 - core)):
            to = (section + side) * 4 + pair
            for ref, lane in ((near_ref, near), (away_ref, away)):
                out_ref[to, :, pl.ds(lane, lanes)] = dot(attended, ref[at]).astype(jnp.bfloat16)


def doubled(value, axes):
    for axis in axes[:-1]:
        value = jnp.concatenate([value, swapped(value, axis)], axis=0)
    return value, swapped(value, axes[-1])


def shards(tokens, w_query, w_keyvalue, cache_keys, cache_values, key_start, key_end, w_out):
    local_rows, width = tokens.shape[1:]
    cache_rows = cache_keys.shape[1]
    kv = lax.axis_index(KV).astype(jnp.int32)
    kv_count = lax.axis_size(KV)
    own = jnp.stack([lax.axis_index("x_hi"), lax.axis_index("core"), kv]).astype(jnp.int32)

    def call(kernel, shapes, name, *operands):
        return pl.pallas_call(
            kernel,
            out_shape=shapes,
            in_specs=[SCALAR] + [WHOLE] * len(operands),
            out_specs=jax.tree.map(lambda _: WHOLE, shapes),
            compiler_params=VMEM,
            name=name,
        )(own, *operands)

    gathered = shared(tokens[0], HEAD)
    query_w = doubled(w_query[None], ("x_hi", *KV))
    pair_w = doubled(w_keyvalue.reshape(1, -1, 2 * width), KV)
    out_w = doubled(w_out[None], ("x_hi", *KV))
    out_w = (*out_w, *(swapped(w, "core") for w in out_w))

    half = jax.ShapeDtypeStruct((2, 4, local_rows, width), jnp.bfloat16)
    keep, send = call(normalize_kernel, (half, half), "normalize", gathered)
    other = swapped(send, "core")
    partial = jax.ShapeDtypeStruct((local_rows, width), jnp.float32)
    mine, theirs = call(query_kernel, (partial, partial), "project_queries", keep, other, *query_w)
    queries = (mine + swapped(theirs, "core")).astype(jnp.bfloat16)
    queries = shared(queries, KV).reshape(-1, width)

    far = swapped(jnp.stack([keep[1], other[1]]), "x_hi")
    partial = jax.ShapeDtypeStruct((2, local_rows, 2 * width), jnp.float32)
    mine, theirs = call(pair_kernel, (partial, partial), "project_pair", keep, other, far, *pair_w)
    mine = mine + swapped(theirs, "core")
    pair = (mine[0] + swapped(mine[1], "x_hi")).astype(jnp.bfloat16)
    place = kv * cache_rows + lax.iota(jnp.int32, cache_rows)
    usable = (place >= key_start[0]) & (place < key_end[0])
    bias = jnp.broadcast_to(jnp.where(usable, 0.0, DEAD).astype(jnp.float32)[None], (8, cache_rows))

    blocks = QUERY_ROWS // local_rows
    padded = local_rows + STAT_ROWS
    parts = pl.pallas_call(
        attend_kernel,
        grid=(width // HD, queries.shape[0] // QUERY_ROWS),
        out_shape=jax.ShapeDtypeStruct((kv_count, padded, width), jnp.bfloat16),
        in_specs=[
            SCALAR,
            pl.BlockSpec((8, cache_rows), lambda h, i: (0, 0)),
            pl.BlockSpec((QUERY_ROWS, HD), lambda h, i: (i, h)),
            pl.BlockSpec((cache_rows, HD), lambda h, i: (0, h)),
            pl.BlockSpec((cache_rows, HD), lambda h, i: (0, h)),
            pl.BlockSpec((local_rows, HD), lambda h, i: (0, h)),
            pl.BlockSpec((local_rows, HD), lambda h, i: (0, h + width // HD)),
        ],
        out_specs=pl.BlockSpec((blocks, padded, HD), lambda h, i: (i, 0, h)),
        scratch_shapes=[pltpu.VMEM((QUERY_ROWS, cache_rows + local_rows), jnp.float32)],
        compiler_params=VMEM,
        name="attend",
    )(kv.reshape(1), bias, queries, cache_keys[0], cache_values[0], pair, pair)

    arrived = lax.all_to_all(parts, KV, split_axis=0, concat_axis=0, tiled=True)
    blocks = jax.ShapeDtypeStruct((lax.axis_size(HEAD), local_rows, width), jnp.bfloat16)
    columns = call(finish_kernel, blocks, "finish", arrived, *out_w)
    columns = lax.all_to_all(columns, HEAD, split_axis=0, concat_axis=0, tiled=True)
    return columns.astype(jnp.float32).sum(axis=0).astype(jnp.bfloat16)[None]


def solution(mesh):
    section, head, kv = (mesh.shape[name] for name in ("section", "head", "kv"))
    torus = Mesh(
        mesh.devices.reshape(section // 2, 2, head // 2, 2, kv // 4, 2, 2),
        ("x_hi", "core", "y", "x_lo", *KV),
    )
    section = ("x_hi", "core")
    rows = (*section, *KV)
    return jax.shard_map(
        shards,
        mesh=torus,
        in_specs=(
            P(section, KV, HEAD),
            P(rows, HEAD),
            P(rows, None, HEAD),
            P(section, KV, HEAD),
            P(section, KV, HEAD),
            P(section),
            P(section),
            P(HEAD, rows),
        ),
        out_specs=P(section, KV, HEAD),
        check_vma=False,
    )
```

```python
import jax
import jax.numpy as jnp
from jax import lax
from jax.experimental import pallas as pl
from jax.experimental.pallas import tpu as pltpu
from jax.sharding import Mesh
from jax.sharding import PartitionSpec as P


HD = 128
HEAD = ("y", "x_lo")
KV = ("z_4", "z_2", "z_1")
STAT_ROWS = 16
QUERY_ROWS = 512
KEY_ROWS = 512
DEAD = -1e30
SCALE = HD**-0.5
EXPONENT = SCALE * 1.4426950408889634
VMEM = pltpu.CompilerParams(vmem_limit_bytes=48 * 1024 * 1024)
SCALAR = pl.BlockSpec(memory_space=pltpu.SMEM)
WHOLE = pl.BlockSpec(memory_space=pltpu.VMEM)


def dot(a, b):
    return jnp.dot(a, b, preferred_element_type=jnp.float32)


def shared(value, axes):
    copies = jnp.broadcast_to(value, (lax.axis_size(axes), *value.shape))
    return lax.all_to_all(copies, axes, split_axis=0, concat_axis=0, tiled=True)


def swapped(value, axis):
    return lax.ppermute(value, axis, [(0, 1), (1, 0)])


def normalize_kernel(place_ref, x_ref, keep_ref, send_ref):
    x_hi, core = place_ref[0], place_ref[1]
    blocks = x_ref.shape[0]
    squares = None
    for b in range(blocks):
        x = x_ref[b].astype(jnp.float32)
        squares = x * x if squares is None else squares + x * x
    mean = jnp.sum(squares, axis=1, keepdims=True) / (blocks * x_ref.shape[2])
    factor = lax.rsqrt(mean + 1e-05)
    for far in range(2):
        half = 1 - x_hi if far else x_hi
        for j in range(4):
            for out_ref, side in ((keep_ref, core), (send_ref, 1 - core)):
                x = x_ref[half * 8 + side * 4 + j].astype(jnp.float32)
                out_ref[far, j] = (x * factor).astype(jnp.bfloat16)


def query_kernel(place_ref, keep_ref, other_ref, w_ref, far_w_ref, own_out, other_out):
    kv = place_ref[2]
    lanes = w_ref.shape[1]
    near = pl.multiple_of((kv & 1) * lanes, lanes)
    away = pl.multiple_of((1 - (kv & 1)) * lanes, lanes)
    total = None
    for at in range(w_ref.shape[0]):
        far, flip_4, flip_2 = at % 2, at // 2 % 2, at // 4
        rows = (kv >> 1) ^ (2 * flip_4 + flip_2)
        for ref, lane in ((w_ref, near), (far_w_ref, away)):
            x = [tile[far, rows, :, pl.ds(lane, lanes)] for tile in (keep_ref, other_ref)]
            part = dot(jnp.concatenate(x, axis=0), ref[at])
            total = part if total is None else total + part
    own_out[...] = total[: own_out.shape[0]]
    other_out[...] = total[own_out.shape[0] :]


def pair_kernel(place_ref, keep_ref, other_ref, far_ref, w_ref, own_out, other_out):
    total = None
    for at in range(w_ref.shape[0]):
        x = [keep_ref[0, at], far_ref[0, at], other_ref[0, at], far_ref[1, at]]
        part = dot(jnp.concatenate(x, axis=0), w_ref[at])
        total = part if total is None else total + part
    rows = own_out.shape[1]
    for n in range(2):
        own_out[n] = total[n * rows : (n + 1) * rows]
        other_out[n] = total[(n + 2) * rows : (n + 3) * rows]


def thirds(value):
    high = value.astype(jnp.bfloat16)
    rest = value - high.astype(jnp.float32)
    middle = rest.astype(jnp.bfloat16)
    low = (rest - middle.astype(jnp.float32)).astype(jnp.bfloat16)
    return [high.astype(jnp.float32), middle.astype(jnp.float32), low.astype(jnp.float32)]


def attend_kernel(kv_ref, bias_ref, q_ref, k_ref, v_ref, new_k_ref, new_v_ref, out_ref, s_ref):
    first = pl.program_id(1) * QUERY_ROWS
    q = q_ref[...]
    cache_rows = k_ref.shape[0]
    new_rows = new_k_ref.shape[0]

    def score(keys):
        return lax.dot_general(q, keys, (((1,), (1,)), ((), ())), preferred_element_type=jnp.float32)

    peak = None
    for at in range(0, cache_rows, KEY_ROWS):
        s = score(k_ref[at : at + KEY_ROWS]) + bias_ref[0:1, at : at + KEY_ROWS]
        s_ref[:, at : at + KEY_ROWS] = s
        for lane in range(0, KEY_ROWS, HD):
            piece = s[:, lane : lane + HD]
            peak = piece if peak is None else jnp.maximum(peak, piece)
    s = score(new_k_ref[...])
    row = first + lax.broadcasted_iota(jnp.int32, s.shape, 0)
    column = kv_ref[0] * new_rows + lax.broadcasted_iota(jnp.int32, s.shape, 1)
    s = jnp.where(column <= row, s, DEAD)
    s_ref[:, cache_rows:] = s
    peak = jnp.max(jnp.maximum(peak, s), axis=1, keepdims=True)

    def mixed(at, values):
        weights = jnp.exp2((s_ref[:, at : at + values.shape[0]] - peak) * EXPONENT)
        both = jnp.concatenate([values, jnp.ones_like(values)], axis=1)
        return dot(weights.astype(jnp.bfloat16), both)

    total = mixed(cache_rows, new_v_ref[...])
    for at in range(0, cache_rows, KEY_ROWS):
        total = total + mixed(at, v_ref[at : at + KEY_ROWS])

    lane = lax.broadcasted_iota(jnp.int32, (HD, HD), 1)
    blocks, rows, _ = out_ref.shape
    own = rows - STAT_ROWS
    for b in range(blocks):
        part = total[b * own : (b + 1) * own]
        out_ref[b, :own] = part[:, :HD].astype(jnp.bfloat16)
        turned = jnp.where(lane == 0, peak[b * own : (b + 1) * own], part[:, HD:]).T
        stats = thirds(turned[0:1]) + thirds(turned[1:2])
        stats = jnp.concatenate([*stats, jnp.zeros((STAT_ROWS - 6, HD), jnp.float32)], axis=0)
        out_ref[b, own:] = stats.astype(jnp.bfloat16)


def finish_kernel(place_ref, parts_ref, w_ref, swap_w_ref, out_ref):
    x_hi, core = place_ref[0], place_ref[1]
    sources, rows, width = parts_ref.shape
    own = rows - STAT_ROWS
    heads = []
    for at in range(0, width, HD):
        stats = [parts_ref[z, own:, at : at + HD].astype(jnp.float32) for z in range(sources)]
        peaks = [s[0:1] + s[1:2] + s[2:3] for s in stats]
        totals = [s[3:4] + s[4:5] + s[5:6] for s in stats]
        highest = peaks[0]
        for p in peaks[1:]:
            highest = jnp.maximum(highest, p)
        factors = [jnp.exp2((p - highest) * EXPONENT) for p in peaks]
        total = sum(f * t for f, t in zip(factors, totals))
        shares = [f / total for f in factors]
        shares = jnp.concatenate([*shares, jnp.zeros((HD - sources, HD), jnp.float32)], axis=0).T
        mixture = None
        for z in range(sources):
            part = parts_ref[z, :own, at : at + HD].astype(jnp.float32) * shares[:, z : z + 1]
            mixture = part if mixture is None else mixture + part
        heads.append(mixture.astype(jnp.bfloat16))
    attended = jnp.concatenate(heads, axis=1)
    lanes = w_ref.shape[3]
    for at in range(w_ref.shape[0]):
        lane = slice(at % 2 * lanes, (at % 2 + 1) * lanes)
        for far in range(2):
            section = 2 * (1 - x_hi if far else x_hi)
            for ref, side in ((w_ref, core), (swap_w_ref, 1 - core)):
                to = (section + side) * 4 + at // 2
                out_ref[to, :, lane] = dot(attended, ref[at, far]).astype(jnp.bfloat16)


def doubled(value, axes):
    for axis in axes[:-1]:
        value = jnp.concatenate([value, swapped(value, axis)], axis=0)
    return value, swapped(value, axes[-1])


def shards(tokens, w_query, w_keyvalue, cache_keys, cache_values, key_start, key_end, w_out):
    local_rows, width = tokens.shape[1:]
    cache_rows = cache_keys.shape[1]
    kv = lax.axis_index(KV).astype(jnp.int32)
    kv_count = lax.axis_size(KV)
    own = jnp.stack([lax.axis_index("x_hi"), lax.axis_index("core"), kv]).astype(jnp.int32)

    def call(kernel, shapes, *operands):
        return pl.pallas_call(
            kernel,
            out_shape=shapes,
            in_specs=[SCALAR] + [WHOLE] * len(operands),
            out_specs=jax.tree.map(lambda _: WHOLE, shapes),
            compiler_params=VMEM,
        )(own, *operands)

    gathered = shared(tokens[0], HEAD)
    query_w = doubled(w_query[None], ("x_hi", *KV))
    pair_w = lax.all_gather(w_keyvalue.reshape(-1, 2 * width), KV, axis=0, tiled=True)
    pair_w = pair_w.reshape(4, -1, 2 * width)
    out_w = jnp.stack([w_out, swapped(w_out, "x_hi")])
    out_w = lax.all_gather(out_w, KV, axis=0, tiled=False)
    out_w = (out_w, swapped(out_w, "core"))

    half = jax.ShapeDtypeStruct((2, 4, local_rows, width), jnp.bfloat16)
    keep, send = call(normalize_kernel, (half, half), gathered)
    other = swapped(send, "core")
    partial = jax.ShapeDtypeStruct((local_rows, width), jnp.float32)
    mine, theirs = call(query_kernel, (partial, partial), keep, other, *query_w)
    queries = (mine + swapped(theirs, "core")).astype(jnp.bfloat16)
    queries = shared(queries, KV).reshape(-1, width)

    far = swapped(jnp.stack([keep[1], other[1]]), "x_hi")
    partial = jax.ShapeDtypeStruct((2, local_rows, 2 * width), jnp.float32)
    mine, theirs = call(pair_kernel, (partial, partial), keep, other, far, pair_w)
    mine = mine + swapped(theirs, "core")
    pair = (mine[0] + swapped(mine[1], "x_hi")).astype(jnp.bfloat16)
    place = kv * cache_rows + lax.iota(jnp.int32, cache_rows)
    usable = (place >= key_start[0]) & (place < key_end[0])
    bias = jnp.broadcast_to(jnp.where(usable, 0.0, DEAD).astype(jnp.float32)[None], (8, cache_rows))

    blocks = QUERY_ROWS // local_rows
    padded = local_rows + STAT_ROWS
    parts = pl.pallas_call(
        attend_kernel,
        grid=(width // HD, queries.shape[0] // QUERY_ROWS),
        out_shape=jax.ShapeDtypeStruct((kv_count, padded, width), jnp.bfloat16),
        in_specs=[
            SCALAR,
            pl.BlockSpec((8, cache_rows), lambda h, i: (0, 0)),
            pl.BlockSpec((QUERY_ROWS, HD), lambda h, i: (i, h)),
            pl.BlockSpec((cache_rows, HD), lambda h, i: (0, h)),
            pl.BlockSpec((cache_rows, HD), lambda h, i: (0, h)),
            pl.BlockSpec((local_rows, HD), lambda h, i: (0, h)),
            pl.BlockSpec((local_rows, HD), lambda h, i: (0, h + width // HD)),
        ],
        out_specs=pl.BlockSpec((blocks, padded, HD), lambda h, i: (i, 0, h)),
        scratch_shapes=[pltpu.VMEM((QUERY_ROWS, cache_rows + local_rows), jnp.float32)],
        compiler_params=VMEM,
        name="attend",
    )(kv.reshape(1), bias, queries, cache_keys[0], cache_values[0], pair, pair)

    arrived = lax.all_to_all(parts, KV, split_axis=0, concat_axis=0, tiled=True)
    blocks = jax.ShapeDtypeStruct((lax.axis_size(HEAD), local_rows, width), jnp.bfloat16)
    columns = call(finish_kernel, blocks, arrived, *out_w)
    columns = lax.all_to_all(columns, HEAD, split_axis=0, concat_axis=0, tiled=True)
    return columns.astype(jnp.float32).sum(axis=0).astype(jnp.bfloat16)[None]


def solution(mesh):
    section, head, kv = (mesh.shape[name] for name in ("section", "head", "kv"))
    torus = Mesh(
        mesh.devices.reshape(section // 2, 2, head // 2, 2, kv // 4, 2, 2),
        ("x_hi", "core", "y", "x_lo", *KV),
    )
    section = ("x_hi", "core")
    rows = (*section, *KV)
    return jax.shard_map(
        shards,
        mesh=torus,
        in_specs=(
            P(section, KV, HEAD),
            P(rows, HEAD),
            P(rows, None, HEAD),
            P(section, KV, HEAD),
            P(section, KV, HEAD),
            P(section),
            P(section),
            P(HEAD, rows),
        ),
        out_specs=P(section, KV, HEAD),
        check_vma=False,
    )
```

```python
import jax
import jax.numpy as jnp
from jax import lax
from jax.experimental import pallas as pl
from jax.experimental.pallas import tpu as pltpu
from jax.sharding import Mesh
from jax.sharding import PartitionSpec as P


HD = 128
HEAD = ("y", "x_lo")
KV = ("z_4", "z_2", "z_1")
STAT_ROWS = 16
QUERY_ROWS = 512
KEY_ROWS = 512
DEAD = -1e30
SCALE = HD**-0.5
EXPONENT = SCALE * 1.4426950408889634
VMEM = pltpu.CompilerParams(vmem_limit_bytes=48 * 1024 * 1024)
SCALAR = pl.BlockSpec(memory_space=pltpu.SMEM)
WHOLE = pl.BlockSpec(memory_space=pltpu.VMEM)


def dot(a, b):
    return jnp.dot(a, b, preferred_element_type=jnp.float32)


def shared(value, axes):
    copies = jnp.broadcast_to(value, (lax.axis_size(axes), *value.shape))
    return lax.all_to_all(copies, axes, split_axis=0, concat_axis=0, tiled=True)


def swapped(value, axis):
    return lax.ppermute(value, axis, [(0, 1), (1, 0)])


def normalize_kernel(place_ref, x_ref, keep_ref, send_ref):
    x_hi, core = place_ref[0], place_ref[1]
    blocks = x_ref.shape[0]
    squares = None
    for b in range(blocks):
        x = x_ref[b].astype(jnp.float32)
        squares = x * x if squares is None else squares + x * x
    mean = jnp.sum(squares, axis=1, keepdims=True) / (blocks * x_ref.shape[2])
    factor = lax.rsqrt(mean + 1e-05)
    for far in range(2):
        half = 1 - x_hi if far else x_hi
        for j in range(4):
            for out_ref, side in ((keep_ref, core), (send_ref, 1 - core)):
                x = x_ref[half * 8 + side * 4 + j].astype(jnp.float32)
                out_ref[far, j] = (x * factor).astype(jnp.bfloat16)


def query_kernel(place_ref, keep_ref, other_ref, w_ref, far_w_ref, away_w_ref, own_out, other_out):
    kv = place_ref[2]
    lanes = far_w_ref.shape[1]
    near = pl.multiple_of((kv & 1) * lanes, lanes)
    away = pl.multiple_of((1 - (kv & 1)) * lanes, lanes)
    total = None
    for at in range(w_ref.shape[0]):
        x = jnp.concatenate([keep_ref[0, at], other_ref[0, at]], axis=0)
        part = dot(x, w_ref[at])
        total = part if total is None else total + part
    for at in range(far_w_ref.shape[0]):
        flip_4, flip_2 = at % 2, at // 2
        rows = (kv >> 1) ^ (2 * flip_4 + flip_2)
        for ref, lane in ((far_w_ref, near), (away_w_ref, away)):
            x = [tile[1, rows, :, pl.ds(lane, lanes)] for tile in (keep_ref, other_ref)]
            total = total + dot(jnp.concatenate(x, axis=0), ref[at])
    own_out[...] = total[: own_out.shape[0]]
    other_out[...] = total[own_out.shape[0] :]


def pair_kernel(place_ref, keep_ref, other_ref, far_ref, w_ref, own_out, other_out):
    total = None
    for at in range(w_ref.shape[0]):
        x = [keep_ref[0, at], far_ref[0, at], other_ref[0, at], far_ref[1, at]]
        part = dot(jnp.concatenate(x, axis=0), w_ref[at])
        total = part if total is None else total + part
    rows = own_out.shape[1]
    for n in range(2):
        own_out[n] = total[n * rows : (n + 1) * rows]
        other_out[n] = total[(n + 2) * rows : (n + 3) * rows]


def thirds(value):
    high = value.astype(jnp.bfloat16)
    rest = value - high.astype(jnp.float32)
    middle = rest.astype(jnp.bfloat16)
    low = (rest - middle.astype(jnp.float32)).astype(jnp.bfloat16)
    return [high.astype(jnp.float32), middle.astype(jnp.float32), low.astype(jnp.float32)]


def score(q, keys):
    return lax.dot_general(q, keys, (((1,), (1,)), ((), ())), preferred_element_type=jnp.float32)


def mixed(scores, peak, values):
    weights = jnp.exp2((scores - peak) * EXPONENT).astype(jnp.bfloat16)
    return dot(weights, jnp.concatenate([values, jnp.ones_like(values)], axis=1))


def cache_kernel(bias_ref, q_ref, k_ref, v_ref, peak_ref, total_ref, s_ref):
    q = q_ref[...]
    cache_rows = k_ref.shape[0]
    peak = None
    for at in range(0, cache_rows, KEY_ROWS):
        s = score(q, k_ref[at : at + KEY_ROWS]) + bias_ref[0:1, at : at + KEY_ROWS]
        s_ref[:, at : at + KEY_ROWS] = s
        for lane in range(0, KEY_ROWS, HD):
            piece = s[:, lane : lane + HD]
            peak = piece if peak is None else jnp.maximum(peak, piece)
    peak = jnp.max(peak, axis=1, keepdims=True)
    total = None
    for at in range(0, cache_rows, KEY_ROWS):
        part = mixed(s_ref[:, at : at + KEY_ROWS], peak, v_ref[at : at + KEY_ROWS])
        total = part if total is None else total + part
    peak_ref[0] = jnp.broadcast_to(peak, peak_ref.shape[1:])
    total_ref[0] = total


def new_kernel(place_ref, q_ref, k_ref, v_ref, peak_ref, total_ref, out_ref):
    s = score(q_ref[...], k_ref[...])
    row = pl.program_id(1) * QUERY_ROWS + lax.broadcasted_iota(jnp.int32, s.shape, 0)
    column = place_ref[2] * k_ref.shape[0] + lax.broadcasted_iota(jnp.int32, s.shape, 1)
    s = jnp.where(column <= row, s, DEAD)
    cache_peak = peak_ref[0]
    peak = jnp.maximum(cache_peak, jnp.max(s, axis=1, keepdims=True))
    fresh = mixed(s, peak, v_ref[...])
    kept = jnp.exp2((cache_peak - peak) * EXPONENT)
    mixture = total_ref[0, :, :HD] * kept + fresh[:, :HD]
    total = total_ref[0, :, HD:] * kept + fresh[:, HD:]

    lane = lax.broadcasted_iota(jnp.int32, (HD, HD), 1)
    blocks, rows, _ = out_ref.shape
    own = rows - STAT_ROWS
    for b in range(blocks):
        part = slice(b * own, (b + 1) * own)
        out_ref[b, :own] = mixture[part].astype(jnp.bfloat16)
        turned = jnp.where(lane == 0, peak[part], total[part]).T
        stats = thirds(turned[0:1]) + thirds(turned[1:2])
        stats = jnp.concatenate([*stats, jnp.zeros((STAT_ROWS - 6, HD), jnp.float32)], axis=0)
        out_ref[b, own:] = stats.astype(jnp.bfloat16)


def finish_kernel(place_ref, parts_ref, w_ref, swap_w_ref, out_ref):
    x_hi, core = place_ref[0], place_ref[1]
    sources, rows, width = parts_ref.shape
    own = rows - STAT_ROWS
    heads = []
    for at in range(0, width, HD):
        stats = [parts_ref[z, own:, at : at + HD].astype(jnp.float32) for z in range(sources)]
        peaks = [s[0:1] + s[1:2] + s[2:3] for s in stats]
        totals = [s[3:4] + s[4:5] + s[5:6] for s in stats]
        highest = peaks[0]
        for p in peaks[1:]:
            highest = jnp.maximum(highest, p)
        factors = [jnp.exp2((p - highest) * EXPONENT) for p in peaks]
        total = sum(f * t for f, t in zip(factors, totals))
        shares = [f / total for f in factors]
        shares = jnp.concatenate([*shares, jnp.zeros((HD - sources, HD), jnp.float32)], axis=0).T
        mixture = None
        for z in range(sources):
            part = parts_ref[z, :own, at : at + HD].astype(jnp.float32) * shares[:, z : z + 1]
            mixture = part if mixture is None else mixture + part
        heads.append(mixture.astype(jnp.bfloat16))
    attended = jnp.concatenate(heads, axis=1)
    lanes = w_ref.shape[3]
    for at in range(w_ref.shape[0]):
        lane = slice(at % 2 * lanes, (at % 2 + 1) * lanes)
        for far in range(2):
            section = 2 * (1 - x_hi if far else x_hi)
            for ref, side in ((w_ref, core), (swap_w_ref, 1 - core)):
                to = (section + side) * 4 + at // 2
                out_ref[to, :, lane] = dot(attended, ref[at, far]).astype(jnp.bfloat16)


def doubled(value, axes):
    for axis in axes[:-1]:
        value = jnp.concatenate([value, swapped(value, axis)], axis=0)
    return value, swapped(value, axes[-1])


def shards(tokens, w_query, w_keyvalue, cache_keys, cache_values, key_start, key_end, w_out):
    local_rows, width = tokens.shape[1:]
    cache_rows = cache_keys.shape[1]
    kv = lax.axis_index(KV).astype(jnp.int32)
    kv_count = lax.axis_size(KV)
    own = jnp.stack([lax.axis_index("x_hi"), lax.axis_index("core"), kv]).astype(jnp.int32)

    def call(kernel, shapes, *operands):
        return pl.pallas_call(
            kernel,
            out_shape=shapes,
            in_specs=[SCALAR] + [WHOLE] * len(operands),
            out_specs=jax.tree.map(lambda _: WHOLE, shapes),
            compiler_params=VMEM,
        )(own, *operands)

    gathered = shared(tokens[0], HEAD)
    query_w_far = swapped(w_query[None], "x_hi")
    out_w = jnp.stack([w_out, swapped(w_out, "x_hi")])
    query_w_far = doubled(query_w_far, KV)
    query_w = shared(w_query, KV).reshape(4, -1, width)
    pair_w = lax.all_gather(w_keyvalue.reshape(-1, 2 * width), KV, axis=0, tiled=True)
    pair_w = pair_w.reshape(4, -1, 2 * width)
    out_w = lax.all_gather(out_w, KV, axis=0, tiled=False)
    out_w = (out_w, swapped(out_w, "core"))

    half = jax.ShapeDtypeStruct((2, 4, local_rows, width), jnp.bfloat16)
    keep, send = call(normalize_kernel, (half, half), gathered)
    other = swapped(send, "core")
    partial = jax.ShapeDtypeStruct((local_rows, width), jnp.float32)
    mine, theirs = call(query_kernel, (partial, partial), keep, other, query_w, *query_w_far)
    queries = (mine + swapped(theirs, "core")).astype(jnp.bfloat16)
    queries = shared(queries, KV).reshape(-1, width)

    far = swapped(jnp.stack([keep[1], other[1]]), "x_hi")
    partial = jax.ShapeDtypeStruct((2, local_rows, 2 * width), jnp.float32)
    mine, theirs = call(pair_kernel, (partial, partial), keep, other, far, pair_w)
    mine = mine + swapped(theirs, "core")
    pair = (mine[0] + swapped(mine[1], "x_hi")).astype(jnp.bfloat16)
    place = kv * cache_rows + lax.iota(jnp.int32, cache_rows)
    usable = (place >= key_start[0]) & (place < key_end[0])
    bias = jnp.broadcast_to(jnp.where(usable, 0.0, DEAD).astype(jnp.float32)[None], (8, cache_rows))

    heads = width // HD
    rows = queries.shape[0]
    grid = (heads, rows // QUERY_ROWS)
    query_spec = pl.BlockSpec((QUERY_ROWS, HD), lambda h, i: (i, h))
    cache_spec = pl.BlockSpec((cache_rows, HD), lambda h, i: (0, h))
    peak_spec = pl.BlockSpec((1, QUERY_ROWS, HD), lambda h, i: (h, i, 0))
    total_spec = pl.BlockSpec((1, QUERY_ROWS, 2 * HD), lambda h, i: (h, i, 0))
    peaks, totals = pl.pallas_call(
        cache_kernel,
        grid=grid,
        out_shape=(
            jax.ShapeDtypeStruct((heads, rows, HD), jnp.float32),
            jax.ShapeDtypeStruct((heads, rows, 2 * HD), jnp.float32),
        ),
        in_specs=[pl.BlockSpec((8, cache_rows), lambda h, i: (0, 0)), query_spec, cache_spec, cache_spec],
        out_specs=(peak_spec, total_spec),
        scratch_shapes=[pltpu.VMEM((QUERY_ROWS, cache_rows), jnp.float32)],
        compiler_params=VMEM,
        name="attend_cache",
    )(bias, queries, cache_keys[0], cache_values[0])
    padded = local_rows + STAT_ROWS
    parts = pl.pallas_call(
        new_kernel,
        grid=grid,
        out_shape=jax.ShapeDtypeStruct((kv_count, padded, width), jnp.bfloat16),
        in_specs=[
            SCALAR,
            query_spec,
            pl.BlockSpec((local_rows, HD), lambda h, i: (0, h)),
            pl.BlockSpec((local_rows, HD), lambda h, i: (0, h + heads)),
            peak_spec,
            total_spec,
        ],
        out_specs=pl.BlockSpec((QUERY_ROWS // local_rows, padded, HD), lambda h, i: (i, 0, h)),
        compiler_params=VMEM,
        name="attend_new",
    )(own, queries, pair, pair, peaks, totals)

    arrived = lax.all_to_all(parts, KV, split_axis=0, concat_axis=0, tiled=True)
    blocks = jax.ShapeDtypeStruct((lax.axis_size(HEAD), local_rows, width), jnp.bfloat16)
    columns = call(finish_kernel, blocks, arrived, *out_w)
    columns = lax.all_to_all(columns, HEAD, split_axis=0, concat_axis=0, tiled=True)
    return columns.astype(jnp.float32).sum(axis=0).astype(jnp.bfloat16)[None]


def solution(mesh):
    section, head, kv = (mesh.shape[name] for name in ("section", "head", "kv"))
    torus = Mesh(
        mesh.devices.reshape(section // 2, 2, head // 2, 2, kv // 4, 2, 2),
        ("x_hi", "core", "y", "x_lo", *KV),
    )
    section = ("x_hi", "core")
    rows = (*section, *KV)
    return jax.shard_map(
        shards,
        mesh=torus,
        in_specs=(
            P(section, KV, HEAD),
            P(rows, HEAD),
            P(rows, None, HEAD),
            P(section, KV, HEAD),
            P(section, KV, HEAD),
            P(section),
            P(section),
            P(HEAD, rows),
        ),
        out_specs=P(section, KV, HEAD),
        check_vma=False,
    )
```

```python
import jax
import jax.numpy as jnp
from jax import lax
from jax.experimental import pallas as pl
from jax.experimental.pallas import tpu as pltpu
from jax.sharding import Mesh
from jax.sharding import PartitionSpec as P


HD = 128
HEAD = ("y", "x_lo")
KV = ("z_4", "z_2", "z_1")
STAT_ROWS = 16
QUERY_ROWS = 512
KEY_ROWS = 512
DEAD = -1e30
SCALE = HD**-0.5
EXPONENT = SCALE * 1.4426950408889634
VMEM = pltpu.CompilerParams(vmem_limit_bytes=48 * 1024 * 1024)
SCALAR = pl.BlockSpec(memory_space=pltpu.SMEM)
WHOLE = pl.BlockSpec(memory_space=pltpu.VMEM)


def dot(a, b):
    return jnp.dot(a, b, preferred_element_type=jnp.float32)


def shared(value, axes):
    copies = jnp.broadcast_to(value, (lax.axis_size(axes), *value.shape))
    return lax.all_to_all(copies, axes, split_axis=0, concat_axis=0, tiled=True)


def swapped(value, axis):
    return lax.ppermute(value, axis, [(0, 1), (1, 0)])


def normalize_kernel(place_ref, x_ref, keep_ref, send_ref):
    x_hi, core = place_ref[0], place_ref[1]
    blocks = x_ref.shape[0]
    squares = None
    for b in range(blocks):
        x = x_ref[b].astype(jnp.float32)
        squares = x * x if squares is None else squares + x * x
    mean = jnp.sum(squares, axis=1, keepdims=True) / (blocks * x_ref.shape[2])
    factor = lax.rsqrt(mean + 1e-05)
    for far in range(2):
        half = 1 - x_hi if far else x_hi
        for j in range(4):
            for out_ref, side in ((keep_ref, core), (send_ref, 1 - core)):
                x = x_ref[half * 8 + side * 4 + j].astype(jnp.float32)
                out_ref[far, j] = (x * factor).astype(jnp.bfloat16)


def both_rows(w_ref, at):
    return jnp.concatenate([w_ref[2 * at], w_ref[2 * at + 1]], axis=0)


def query_kernel(place_ref, keep_ref, other_ref, w_ref, far_w_ref, away_w_ref, own_out, other_out):
    kv = place_ref[2]
    lanes = far_w_ref.shape[1]
    near = pl.multiple_of((kv & 1) * lanes, lanes)
    away = pl.multiple_of((1 - (kv & 1)) * lanes, lanes)
    total = None
    for at in range(w_ref.shape[0] // 2):
        x = jnp.concatenate([keep_ref[0, at], other_ref[0, at]], axis=0)
        part = dot(x, both_rows(w_ref, at))
        total = part if total is None else total + part
    for at in range(far_w_ref.shape[0]):
        flip_4, flip_2 = at % 2, at // 2
        rows = (kv >> 1) ^ (2 * flip_4 + flip_2)
        for ref, lane in ((far_w_ref, near), (away_w_ref, away)):
            x = [tile[1, rows, :, pl.ds(lane, lanes)] for tile in (keep_ref, other_ref)]
            total = total + dot(jnp.concatenate(x, axis=0), ref[at])
    own_out[...] = total[: own_out.shape[0]]
    other_out[...] = total[own_out.shape[0] :]


def pair_kernel(place_ref, keep_ref, other_ref, far_ref, key_w_ref, value_w_ref, own_out, other_out):
    rows, width = own_out.shape[1], key_w_ref.shape[2]
    for lane, w_ref in ((0, key_w_ref), (width, value_w_ref)):
        total = None
        for at in range(w_ref.shape[0] // 2):
            x = [keep_ref[0, at], far_ref[0, at], other_ref[0, at], far_ref[1, at]]
            part = dot(jnp.concatenate(x, axis=0), both_rows(w_ref, at))
            total = part if total is None else total + part
        for n in range(2):
            own_out[n, :, lane : lane + width] = total[n * rows : (n + 1) * rows]
            other_out[n, :, lane : lane + width] = total[(n + 2) * rows : (n + 3) * rows]


def thirds(value):
    high = value.astype(jnp.bfloat16)
    rest = value - high.astype(jnp.float32)
    middle = rest.astype(jnp.bfloat16)
    low = (rest - middle.astype(jnp.float32)).astype(jnp.bfloat16)
    return [high.astype(jnp.float32), middle.astype(jnp.float32), low.astype(jnp.float32)]


def score(q, keys):
    return lax.dot_general(q, keys, (((1,), (1,)), ((), ())), preferred_element_type=jnp.float32)


def mixed(scores, peak, values):
    weights = jnp.exp2((scores - peak) * EXPONENT).astype(jnp.bfloat16)
    return dot(weights, jnp.concatenate([values, jnp.ones_like(values)], axis=1))


def cache_kernel(bias_ref, q_ref, k_ref, v_ref, peak_ref, total_ref, s_ref):
    q = q_ref[...]
    cache_rows = k_ref.shape[0]
    peak = None
    for at in range(0, cache_rows, KEY_ROWS):
        s = score(q, k_ref[at : at + KEY_ROWS]) + bias_ref[0:1, at : at + KEY_ROWS]
        s_ref[:, at : at + KEY_ROWS] = s
        for lane in range(0, KEY_ROWS, HD):
            piece = s[:, lane : lane + HD]
            peak = piece if peak is None else jnp.maximum(peak, piece)
    peak = jnp.max(peak, axis=1, keepdims=True)
    total = None
    for at in range(0, cache_rows, KEY_ROWS):
        part = mixed(s_ref[:, at : at + KEY_ROWS], peak, v_ref[at : at + KEY_ROWS])
        total = part if total is None else total + part
    peak_ref[0] = jnp.broadcast_to(peak, peak_ref.shape[1:])
    total_ref[0] = total


def new_kernel(place_ref, q_ref, k_ref, v_ref, peak_ref, total_ref, out_ref):
    s = score(q_ref[...], k_ref[...])
    row = pl.program_id(1) * QUERY_ROWS + lax.broadcasted_iota(jnp.int32, s.shape, 0)
    column = place_ref[2] * k_ref.shape[0] + lax.broadcasted_iota(jnp.int32, s.shape, 1)
    s = jnp.where(column <= row, s, DEAD)
    cache_peak = peak_ref[0]
    peak = jnp.maximum(cache_peak, jnp.max(s, axis=1, keepdims=True))
    fresh = mixed(s, peak, v_ref[...])
    kept = jnp.exp2((cache_peak - peak) * EXPONENT)
    mixture = total_ref[0, :, :HD] * kept + fresh[:, :HD]
    total = total_ref[0, :, HD:] * kept + fresh[:, HD:]

    lane = lax.broadcasted_iota(jnp.int32, (HD, HD), 1)
    blocks, rows, _ = out_ref.shape
    own = rows - STAT_ROWS
    for b in range(blocks):
        part = slice(b * own, (b + 1) * own)
        out_ref[b, :own] = mixture[part].astype(jnp.bfloat16)
        turned = jnp.where(lane == 0, peak[part], total[part]).T
        stats = thirds(turned[0:1]) + thirds(turned[1:2])
        stats = jnp.concatenate([*stats, jnp.zeros((STAT_ROWS - 6, HD), jnp.float32)], axis=0)
        out_ref[b, own:] = stats.astype(jnp.bfloat16)


def finish_kernel(place_ref, parts_ref, w_ref, far_w_ref, swap_w_ref, swap_far_w_ref, out_ref):
    x_hi, core = place_ref[0], place_ref[1]
    sources, rows, width = parts_ref.shape
    own = rows - STAT_ROWS
    heads = []
    for at in range(0, width, HD):
        stats = [parts_ref[z, own:, at : at + HD].astype(jnp.float32) for z in range(sources)]
        peaks = [s[0:1] + s[1:2] + s[2:3] for s in stats]
        totals = [s[3:4] + s[4:5] + s[5:6] for s in stats]
        highest = peaks[0]
        for p in peaks[1:]:
            highest = jnp.maximum(highest, p)
        factors = [jnp.exp2((p - highest) * EXPONENT) for p in peaks]
        total = sum(f * t for f, t in zip(factors, totals))
        shares = [f / total for f in factors]
        shares = jnp.concatenate([*shares, jnp.zeros((HD - sources, HD), jnp.float32)], axis=0).T
        mixture = None
        for z in range(sources):
            part = parts_ref[z, :own, at : at + HD].astype(jnp.float32) * shares[:, z : z + 1]
            mixture = part if mixture is None else mixture + part
        heads.append(mixture.astype(jnp.bfloat16))
    attended = jnp.concatenate(heads, axis=1)
    lanes = w_ref.shape[1]
    sides = ((w_ref, x_hi, core), (far_w_ref, 1 - x_hi, core))
    sides += ((swap_w_ref, x_hi, 1 - core), (swap_far_w_ref, 1 - x_hi, 1 - core))
    for at in range(w_ref.shape[0]):
        lane = slice(at % 2 * lanes, (at % 2 + 1) * lanes)
        for ref, half, side in sides:
            w = jnp.concatenate([ref[at, :, :lanes], ref[at, :, lanes:]], axis=0)
            to = (2 * half + side) * 4 + at // 2
            out_ref[to, :, lane] = dot(attended, w).astype(jnp.bfloat16)


def doubled(value, axes):
    for axis in axes[:-1]:
        value = jnp.concatenate([value, swapped(value, axis)], axis=0)
    return value, swapped(value, axes[-1])


def shards(tokens, w_query, w_keyvalue, cache_keys, cache_values, key_start, key_end, w_out):
    local_rows, width = tokens.shape[1:]
    cache_rows = cache_keys.shape[1]
    kv = lax.axis_index(KV).astype(jnp.int32)
    kv_count = lax.axis_size(KV)
    own = jnp.stack([lax.axis_index("x_hi"), lax.axis_index("core"), kv]).astype(jnp.int32)

    def part_of_weights(index):
        block = (kv_count, local_rows, width)
        operand = pltpu.with_memory_space_constraint(weights, pltpu.HBM)
        return pl.BlockSpec(block, lambda i: (0, index, 0)), operand

    def call(kernel, shapes, *operands):
        pairs = [o if isinstance(o, tuple) else (WHOLE, o) for o in operands]
        return pl.pallas_call(
            kernel,
            grid=(1,),
            out_shape=shapes,
            in_specs=[SCALAR] + [spec for spec, _ in pairs],
            out_specs=jax.tree.map(lambda _: WHOLE, shapes),
            compiler_params=VMEM,
        )(own, *(operand for _, operand in pairs))

    gathered = shared(tokens[0], HEAD)
    query_w_far = swapped(w_query[None], "x_hi")
    query_w_far = doubled(query_w_far, KV)
    out_w = jnp.concatenate([w_out[:local_rows], w_out[local_rows:]], axis=1)
    weights = jnp.concatenate([w_query, w_keyvalue[:, 0], w_keyvalue[:, 1], out_w], axis=0)
    weights = lax.all_gather(weights, KV, axis=0, tiled=False)
    out_w = weights[:, 3 * local_rows :]
    out_w_far = swapped(out_w, "x_hi")
    out_w_core = swapped(out_w, "core")
    out_w_both = swapped(out_w_far, "core")

    half = jax.ShapeDtypeStruct((2, 4, local_rows, width), jnp.bfloat16)
    keep, send = call(normalize_kernel, (half, half), gathered)
    other = swapped(send, "core")
    partial = jax.ShapeDtypeStruct((local_rows, width), jnp.float32)
    mine, theirs = call(query_kernel, (partial, partial), keep, other, part_of_weights(0), *query_w_far)
    queries = (mine + swapped(theirs, "core")).astype(jnp.bfloat16)
    queries = shared(queries, KV).reshape(-1, width)

    far = swapped(jnp.stack([keep[1], other[1]]), "x_hi")
    partial = jax.ShapeDtypeStruct((2, local_rows, 2 * width), jnp.float32)
    mine, theirs = call(pair_kernel, (partial, partial), keep, other, far, part_of_weights(1), part_of_weights(2))
    mine = mine + swapped(theirs, "core")
    pair = (mine[0] + swapped(mine[1], "x_hi")).astype(jnp.bfloat16)
    place = kv * cache_rows + lax.iota(jnp.int32, cache_rows)
    usable = (place >= key_start[0]) & (place < key_end[0])
    bias = jnp.broadcast_to(jnp.where(usable, 0.0, DEAD).astype(jnp.float32)[None], (8, cache_rows))

    heads = width // HD
    rows = queries.shape[0]
    grid = (heads, rows // QUERY_ROWS)
    query_spec = pl.BlockSpec((QUERY_ROWS, HD), lambda h, i: (i, h))
    cache_spec = pl.BlockSpec((cache_rows, HD), lambda h, i: (0, h))
    peak_spec = pl.BlockSpec((1, QUERY_ROWS, HD), lambda h, i: (h, i, 0))
    total_spec = pl.BlockSpec((1, QUERY_ROWS, 2 * HD), lambda h, i: (h, i, 0))
    peaks, totals = pl.pallas_call(
        cache_kernel,
        grid=grid,
        out_shape=(
            jax.ShapeDtypeStruct((heads, rows, HD), jnp.float32),
            jax.ShapeDtypeStruct((heads, rows, 2 * HD), jnp.float32),
        ),
        in_specs=[pl.BlockSpec((8, cache_rows), lambda h, i: (0, 0)), query_spec, cache_spec, cache_spec],
        out_specs=(peak_spec, total_spec),
        scratch_shapes=[pltpu.VMEM((QUERY_ROWS, cache_rows), jnp.float32)],
        compiler_params=VMEM,
        name="attend_cache",
    )(bias, queries, cache_keys[0], cache_values[0])
    padded = local_rows + STAT_ROWS
    parts = pl.pallas_call(
        new_kernel,
        grid=grid,
        out_shape=jax.ShapeDtypeStruct((kv_count, padded, width), jnp.bfloat16),
        in_specs=[
            SCALAR,
            query_spec,
            pl.BlockSpec((local_rows, HD), lambda h, i: (0, h)),
            pl.BlockSpec((local_rows, HD), lambda h, i: (0, h + heads)),
            peak_spec,
            total_spec,
        ],
        out_specs=pl.BlockSpec((QUERY_ROWS // local_rows, padded, HD), lambda h, i: (i, 0, h)),
        compiler_params=VMEM,
        name="attend_new",
    )(own, queries, pair, pair, peaks, totals)

    arrived = lax.all_to_all(parts, KV, split_axis=0, concat_axis=0, tiled=True)
    blocks = jax.ShapeDtypeStruct((lax.axis_size(HEAD), local_rows, width), jnp.bfloat16)
    columns = call(finish_kernel, blocks, arrived, out_w, out_w_far, out_w_core, out_w_both)
    columns = lax.all_to_all(columns, HEAD, split_axis=0, concat_axis=0, tiled=True)
    return columns.astype(jnp.float32).sum(axis=0).astype(jnp.bfloat16)[None]


def solution(mesh):
    section, head, kv = (mesh.shape[name] for name in ("section", "head", "kv"))
    torus = Mesh(
        mesh.devices.reshape(section // 2, 2, head // 2, 2, kv // 4, 2, 2),
        ("x_hi", "core", "y", "x_lo", *KV),
    )
    section = ("x_hi", "core")
    rows = (*section, *KV)
    return jax.shard_map(
        shards,
        mesh=torus,
        in_specs=(
            P(section, KV, HEAD),
            P(rows, HEAD),
            P(rows, None, HEAD),
            P(section, KV, HEAD),
            P(section, KV, HEAD),
            P(section),
            P(section),
            P(HEAD, rows),
        ),
        out_specs=P(section, KV, HEAD),
        check_vma=False,
    )
```

```python
import jax
import jax.numpy as jnp
from jax import lax
from jax.experimental import pallas as pl
from jax.experimental.pallas import tpu as pltpu
from jax.sharding import Mesh
from jax.sharding import PartitionSpec as P


HD = 128
HEAD = ("y", "x_lo")
KV = ("z_4", "z_2", "z_1")
STAT_ROWS = 16
QUERY_ROWS = 512
KEY_ROWS = 512
DEAD = -1e30
SCALE = HD**-0.5
EXPONENT = SCALE * 1.4426950408889634
VMEM = pltpu.CompilerParams(vmem_limit_bytes=48 * 1024 * 1024)
SCALAR = pl.BlockSpec(memory_space=pltpu.SMEM)
WHOLE = pl.BlockSpec(memory_space=pltpu.VMEM)


def dot(a, b):
    return jnp.dot(a, b, preferred_element_type=jnp.float32)


def shared(value, axes):
    copies = jnp.broadcast_to(value, (lax.axis_size(axes), *value.shape))
    return lax.all_to_all(copies, axes, split_axis=0, concat_axis=0, tiled=True)


def swapped(value, axis):
    return lax.ppermute(value, axis, [(0, 1), (1, 0)])


def normalize_kernel(place_ref, x_ref, keep_ref, send_ref):
    x_hi, core = place_ref[0], place_ref[1]
    blocks = x_ref.shape[0]
    squares = None
    for b in range(blocks):
        x = x_ref[b].astype(jnp.float32)
        squares = x * x if squares is None else squares + x * x
    mean = jnp.sum(squares, axis=1, keepdims=True) / (blocks * x_ref.shape[2])
    factor = lax.rsqrt(mean + 1e-05)
    for far in range(2):
        half = 1 - x_hi if far else x_hi
        for j in range(4):
            for out_ref, side in ((keep_ref, core), (send_ref, 1 - core)):
                x = x_ref[half * 8 + side * 4 + j].astype(jnp.float32)
                out_ref[far, j] = (x * factor).astype(jnp.bfloat16)


def both_rows(w_ref, at):
    return jnp.concatenate([w_ref[2 * at], w_ref[2 * at + 1]], axis=0)


def query_kernel(place_ref, keep_ref, other_ref, w_ref, far_w_ref, away_w_ref, own_out, other_out):
    kv = place_ref[2]
    lanes = far_w_ref.shape[1]
    near = pl.multiple_of((kv & 1) * lanes, lanes)
    away = pl.multiple_of((1 - (kv & 1)) * lanes, lanes)
    total = None
    for at in range(w_ref.shape[0] // 2):
        x = jnp.concatenate([keep_ref[0, at], other_ref[0, at]], axis=0)
        part = dot(x, both_rows(w_ref, at))
        total = part if total is None else total + part
    for at in range(far_w_ref.shape[0]):
        flip_4, flip_2 = at % 2, at // 2
        rows = (kv >> 1) ^ (2 * flip_4 + flip_2)
        for ref, lane in ((far_w_ref, near), (away_w_ref, away)):
            x = [tile[1, rows, :, pl.ds(lane, lanes)] for tile in (keep_ref, other_ref)]
            total = total + dot(jnp.concatenate(x, axis=0), ref[at])
    own_out[...] = total[: own_out.shape[0]]
    other_out[...] = total[own_out.shape[0] :]


def pair_kernel(place_ref, keep_ref, other_ref, far_ref, key_w_ref, value_w_ref, near_out, far_out, other_out):
    rows, width = near_out.shape[0], key_w_ref.shape[2]
    outs = (near_out, far_out, other_out.at[0], other_out.at[1])
    for lane, w_ref in ((0, key_w_ref), (width, value_w_ref)):
        total = None
        for at in range(w_ref.shape[0] // 2):
            x = [keep_ref[0, at], far_ref[0, at], other_ref[0, at], far_ref[1, at]]
            part = dot(jnp.concatenate(x, axis=0), both_rows(w_ref, at))
            total = part if total is None else total + part
        for n, out_ref in enumerate(outs):
            out_ref[:, lane : lane + width] = total[n * rows : (n + 1) * rows]


def copies_kernel(place_ref, own_ref, other_ref, out_ref):
    total = (own_ref[...] + other_ref[...]).astype(jnp.bfloat16)
    for n in range(out_ref.shape[0]):
        out_ref[n] = total


def pack_kernel(place_ref, query_ref, pair_ref, out_w_ref, out_ref):
    rows = query_ref.shape[0]
    out_ref[:rows] = query_ref[...]
    out_ref[rows : 2 * rows] = pair_ref[:, 0]
    out_ref[2 * rows : 3 * rows] = pair_ref[:, 1]
    out_ref[3 * rows :] = jnp.concatenate([out_w_ref[:rows], out_w_ref[rows:]], axis=1)


def thirds(value):
    high = value.astype(jnp.bfloat16)
    rest = value - high.astype(jnp.float32)
    middle = rest.astype(jnp.bfloat16)
    low = (rest - middle.astype(jnp.float32)).astype(jnp.bfloat16)
    return [high.astype(jnp.float32), middle.astype(jnp.float32), low.astype(jnp.float32)]


def score(q, keys):
    return lax.dot_general(q, keys, (((1,), (1,)), ((), ())), preferred_element_type=jnp.float32)


def mixed(scores, peak, values):
    weights = jnp.exp2((scores - peak) * EXPONENT).astype(jnp.bfloat16)
    return dot(weights, jnp.concatenate([values, jnp.ones_like(values)], axis=1))


def cache_kernel(bias_ref, q_ref, k_ref, v_ref, peak_ref, total_ref, s_ref):
    q = q_ref[...]
    cache_rows = k_ref.shape[0]
    peak = None
    for at in range(0, cache_rows, KEY_ROWS):
        s = score(q, k_ref[at : at + KEY_ROWS]) + bias_ref[0:1, at : at + KEY_ROWS]
        s_ref[:, at : at + KEY_ROWS] = s
        for lane in range(0, KEY_ROWS, HD):
            piece = s[:, lane : lane + HD]
            peak = piece if peak is None else jnp.maximum(peak, piece)
    peak = jnp.max(peak, axis=1, keepdims=True)
    total = None
    for at in range(0, cache_rows, KEY_ROWS):
        part = mixed(s_ref[:, at : at + KEY_ROWS], peak, v_ref[at : at + KEY_ROWS])
        total = part if total is None else total + part
    peak_ref[0] = jnp.broadcast_to(peak, peak_ref.shape[1:])
    total_ref[0] = total


def new_kernel(place_ref, q_ref, *refs):
    *pair_refs, peak_ref, total_ref, out_ref = refs
    keys, values = [
        (near[...] + core[0] + far[...]).astype(jnp.bfloat16) for near, core, far in (pair_refs[:3], pair_refs[3:])
    ]
    s = score(q_ref[...], keys)
    row = pl.program_id(1) * QUERY_ROWS + lax.broadcasted_iota(jnp.int32, s.shape, 0)
    column = place_ref[2] * keys.shape[0] + lax.broadcasted_iota(jnp.int32, s.shape, 1)
    s = jnp.where(column <= row, s, DEAD)
    cache_peak = peak_ref[0]
    peak = jnp.maximum(cache_peak, jnp.max(s, axis=1, keepdims=True))
    fresh = mixed(s, peak, values)
    kept = jnp.exp2((cache_peak - peak) * EXPONENT)
    mixture = total_ref[0, :, :HD] * kept + fresh[:, :HD]
    total = total_ref[0, :, HD:] * kept + fresh[:, HD:]

    lane = lax.broadcasted_iota(jnp.int32, (HD, HD), 1)
    blocks, rows, _ = out_ref.shape
    own = rows - STAT_ROWS
    for b in range(blocks):
        part = slice(b * own, (b + 1) * own)
        out_ref[b, :own] = mixture[part].astype(jnp.bfloat16)
        turned = jnp.where(lane == 0, peak[part], total[part]).T
        stats = thirds(turned[0:1]) + thirds(turned[1:2])
        stats = jnp.concatenate([*stats, jnp.zeros((STAT_ROWS - 6, HD), jnp.float32)], axis=0)
        out_ref[b, own:] = stats.astype(jnp.bfloat16)


def finish_kernel(place_ref, parts_ref, w_ref, far_w_ref, swap_w_ref, swap_far_w_ref, out_ref):
    x_hi, core = place_ref[0], place_ref[1]
    sources, rows, width = parts_ref.shape
    own = rows - STAT_ROWS
    heads = []
    for at in range(0, width, HD):
        stats = [parts_ref[z, own:, at : at + HD].astype(jnp.float32) for z in range(sources)]
        peaks = [s[0:1] + s[1:2] + s[2:3] for s in stats]
        totals = [s[3:4] + s[4:5] + s[5:6] for s in stats]
        highest = peaks[0]
        for p in peaks[1:]:
            highest = jnp.maximum(highest, p)
        factors = [jnp.exp2((p - highest) * EXPONENT) for p in peaks]
        total = sum(f * t for f, t in zip(factors, totals))
        shares = [f / total for f in factors]
        shares = jnp.concatenate([*shares, jnp.zeros((HD - sources, HD), jnp.float32)], axis=0).T
        mixture = None
        for z in range(sources):
            part = parts_ref[z, :own, at : at + HD].astype(jnp.float32) * shares[:, z : z + 1]
            mixture = part if mixture is None else mixture + part
        heads.append(mixture.astype(jnp.bfloat16))
    attended = jnp.concatenate(heads, axis=1)
    lanes = w_ref.shape[1]
    sides = ((w_ref, x_hi, core), (far_w_ref, 1 - x_hi, core))
    sides += ((swap_w_ref, x_hi, 1 - core), (swap_far_w_ref, 1 - x_hi, 1 - core))
    for at in range(w_ref.shape[0]):
        lane = slice(at % 2 * lanes, (at % 2 + 1) * lanes)
        for ref, half, side in sides:
            w = jnp.concatenate([ref[at, :, :lanes], ref[at, :, lanes:]], axis=0)
            to = (2 * half + side) * 4 + at // 2
            out_ref[to, :, lane] = dot(attended, w).astype(jnp.bfloat16)


def doubled(value, axes):
    for axis in axes[:-1]:
        value = jnp.concatenate([value, swapped(value, axis)], axis=0)
    return value, swapped(value, axes[-1])


def shards(tokens, w_query, w_keyvalue, cache_keys, cache_values, key_start, key_end, w_out):
    local_rows, width = tokens.shape[1:]
    cache_rows = cache_keys.shape[1]
    kv = lax.axis_index(KV).astype(jnp.int32)
    kv_count = lax.axis_size(KV)
    own = jnp.stack([lax.axis_index("x_hi"), lax.axis_index("core"), kv]).astype(jnp.int32)

    def part_of_weights(index):
        block = (kv_count, local_rows, width)
        operand = pltpu.with_memory_space_constraint(weights, pltpu.HBM)
        return pl.BlockSpec(block, lambda i: (0, index, 0)), operand

    def call(kernel, shapes, *operands):
        pairs = [o if isinstance(o, tuple) else (WHOLE, o) for o in operands]
        return pl.pallas_call(
            kernel,
            grid=(1,),
            out_shape=shapes,
            in_specs=[SCALAR] + [spec for spec, _ in pairs],
            out_specs=jax.tree.map(lambda _: WHOLE, shapes),
            compiler_params=VMEM,
        )(own, *(operand for _, operand in pairs))

    gathered = shared(tokens[0], HEAD)
    query_w_far = swapped(w_query[None], "x_hi")
    query_w_far = doubled(query_w_far, KV)
    packed = jax.ShapeDtypeStruct((4 * local_rows, width), jnp.bfloat16)
    weights = call(pack_kernel, packed, w_query, w_keyvalue, w_out)
    weights = lax.all_gather(weights, KV, axis=0, tiled=False)
    out_w = weights[:, 3 * local_rows :]
    out_w_far = swapped(out_w, "x_hi")
    out_w_core = swapped(out_w, "core")
    out_w_both = swapped(out_w_far, "core")

    half = jax.ShapeDtypeStruct((2, 4, local_rows, width), jnp.bfloat16)
    keep, send = call(normalize_kernel, (half, half), gathered)
    other = swapped(send, "core")
    partial = jax.ShapeDtypeStruct((local_rows, width), jnp.float32)
    mine, theirs = call(query_kernel, (partial, partial), keep, other, part_of_weights(0), *query_w_far)
    copies = jax.ShapeDtypeStruct((kv_count, local_rows, width), jnp.bfloat16)
    copies = call(copies_kernel, copies, mine, swapped(theirs, "core"))
    queries = lax.all_to_all(copies, KV, split_axis=0, concat_axis=0, tiled=True)
    queries = queries.reshape(-1, width)

    far = swapped(jnp.stack([keep[1], other[1]]), "x_hi")
    partial = jax.ShapeDtypeStruct((local_rows, 2 * width), jnp.float32)
    both = jax.ShapeDtypeStruct((2, local_rows, 2 * width), jnp.float32)
    pair_near, pair_far, theirs = call(
        pair_kernel,
        (partial, partial, both),
        keep,
        other,
        far,
        part_of_weights(1),
        part_of_weights(2),
    )
    pair_core = swapped(theirs, "core")
    pair_far = swapped(pair_far + pair_core[1], "x_hi")
    place = kv * cache_rows + lax.iota(jnp.int32, cache_rows)
    usable = (place >= key_start[0]) & (place < key_end[0])
    bias = jnp.broadcast_to(jnp.where(usable, 0.0, DEAD).astype(jnp.float32)[None], (8, cache_rows))

    heads = width // HD
    rows = queries.shape[0]
    grid = (heads, rows // QUERY_ROWS)
    query_spec = pl.BlockSpec((QUERY_ROWS, HD), lambda h, i: (i, h))
    cache_spec = pl.BlockSpec((cache_rows, HD), lambda h, i: (0, h))
    peak_spec = pl.BlockSpec((1, QUERY_ROWS, HD), lambda h, i: (h, i, 0))
    total_spec = pl.BlockSpec((1, QUERY_ROWS, 2 * HD), lambda h, i: (h, i, 0))
    peaks, totals = pl.pallas_call(
        cache_kernel,
        grid=grid,
        out_shape=(
            jax.ShapeDtypeStruct((heads, rows, HD), jnp.float32),
            jax.ShapeDtypeStruct((heads, rows, 2 * HD), jnp.float32),
        ),
        in_specs=[pl.BlockSpec((8, cache_rows), lambda h, i: (0, 0)), query_spec, cache_spec, cache_spec],
        out_specs=(peak_spec, total_spec),
        scratch_shapes=[pltpu.VMEM((QUERY_ROWS, cache_rows), jnp.float32)],
        compiler_params=VMEM,
        name="attend_cache",
    )(bias, queries, cache_keys[0], cache_values[0])

    def pair_specs(first):
        flat = pl.BlockSpec((local_rows, HD), lambda h, i: (0, h + first))
        return flat, pl.BlockSpec((1, local_rows, HD), lambda h, i: (0, 0, h + first)), flat

    padded = local_rows + STAT_ROWS
    parts = pl.pallas_call(
        new_kernel,
        grid=grid,
        out_shape=jax.ShapeDtypeStruct((kv_count, padded, width), jnp.bfloat16),
        in_specs=[
            SCALAR,
            query_spec,
            *pair_specs(0),
            *pair_specs(heads),
            peak_spec,
            total_spec,
        ],
        out_specs=pl.BlockSpec((QUERY_ROWS // local_rows, padded, HD), lambda h, i: (i, 0, h)),
        compiler_params=VMEM,
        name="attend_new",
    )(own, queries, *(pair_near, pair_core, pair_far) * 2, peaks, totals)

    arrived = lax.all_to_all(parts, KV, split_axis=0, concat_axis=0, tiled=True)
    blocks = jax.ShapeDtypeStruct((lax.axis_size(HEAD), local_rows, width), jnp.bfloat16)
    columns = call(finish_kernel, blocks, arrived, out_w, out_w_far, out_w_core, out_w_both)
    columns = lax.all_to_all(columns, HEAD, split_axis=0, concat_axis=0, tiled=True)
    return columns.astype(jnp.float32).sum(axis=0).astype(jnp.bfloat16)[None]


def solution(mesh):
    section, head, kv = (mesh.shape[name] for name in ("section", "head", "kv"))
    torus = Mesh(
        mesh.devices.reshape(section // 2, 2, head // 2, 2, kv // 4, 2, 2),
        ("x_hi", "core", "y", "x_lo", *KV),
    )
    section = ("x_hi", "core")
    rows = (*section, *KV)
    return jax.shard_map(
        shards,
        mesh=torus,
        in_specs=(
            P(section, KV, HEAD),
            P(rows, HEAD),
            P(rows, None, HEAD),
            P(section, KV, HEAD),
            P(section, KV, HEAD),
            P(section),
            P(section),
            P(HEAD, rows),
        ),
        out_specs=P(section, KV, HEAD),
        check_vma=False,
    )
```

```python
import jax
import jax.numpy as jnp
from jax import lax
from jax.experimental import pallas as pl
from jax.experimental.pallas import tpu as pltpu
from jax.sharding import Mesh
from jax.sharding import PartitionSpec as P


HD = 128
HEAD = ("y", "x_lo")
KV = ("z_4", "z_2", "z_1")
STAT_ROWS = 16
QUERY_ROWS = 512
KEY_ROWS = 512
DEAD = -1e30
SCALE = HD**-0.5
EXPONENT = SCALE * 1.4426950408889634
VMEM = pltpu.CompilerParams(vmem_limit_bytes=48 * 1024 * 1024)
SCALAR = pl.BlockSpec(memory_space=pltpu.SMEM)
WHOLE = pl.BlockSpec(memory_space=pltpu.VMEM)


def dot(a, b):
    return jnp.dot(a, b, preferred_element_type=jnp.float32)


def shared(value, axes):
    copies = jnp.broadcast_to(value, (lax.axis_size(axes), *value.shape))
    return lax.all_to_all(copies, axes, split_axis=0, concat_axis=0, tiled=True)


def swapped(value, axis):
    return lax.ppermute(value, axis, [(0, 1), (1, 0)])


def normalize_kernel(place_ref, x_ref, keep_ref, send_ref):
    x_hi, core = place_ref[0], place_ref[1]
    blocks = x_ref.shape[0]
    squares = None
    for b in range(blocks):
        x = x_ref[b].astype(jnp.float32)
        squares = x * x if squares is None else squares + x * x
    mean = jnp.sum(squares, axis=1, keepdims=True) / (blocks * x_ref.shape[2])
    factor = lax.rsqrt(mean + 1e-05)
    for far in range(2):
        half = 1 - x_hi if far else x_hi
        for j in range(4):
            for out_ref, side in ((keep_ref, core), (send_ref, 1 - core)):
                x = x_ref[half * 8 + side * 4 + j].astype(jnp.float32)
                out_ref[far, j] = (x * factor).astype(jnp.bfloat16)


def both_rows(w_ref, at):
    return jnp.concatenate([w_ref[2 * at], w_ref[2 * at + 1]], axis=0)


def query_kernel(place_ref, keep_ref, other_ref, w_ref, far_w_ref, away_w_ref, own_out, other_out):
    kv = place_ref[2]
    lanes = far_w_ref.shape[1]
    near = pl.multiple_of((kv & 1) * lanes, lanes)
    away = pl.multiple_of((1 - (kv & 1)) * lanes, lanes)
    total = None
    for at in range(w_ref.shape[0] // 2):
        x = jnp.concatenate([keep_ref[0, at], other_ref[0, at]], axis=0)
        part = dot(x, both_rows(w_ref, at))
        total = part if total is None else total + part
    for at in range(far_w_ref.shape[0]):
        flip_4, flip_2 = at % 2, at // 2
        rows = (kv >> 1) ^ (2 * flip_4 + flip_2)
        for ref, lane in ((far_w_ref, near), (away_w_ref, away)):
            x = [tile[1, rows, :, pl.ds(lane, lanes)] for tile in (keep_ref, other_ref)]
            total = total + dot(jnp.concatenate(x, axis=0), ref[at])
    own_out[...] = total[: own_out.shape[0]]
    other_out[...] = total[own_out.shape[0] :]


def pair_kernel(place_ref, keep_ref, other_ref, far_ref, key_w_ref, value_w_ref, near_out, far_out, other_out):
    rows, width = near_out.shape[0], key_w_ref.shape[2]
    outs = (near_out, far_out, other_out.at[0], other_out.at[1])
    for lane, w_ref in ((0, key_w_ref), (width, value_w_ref)):
        total = None
        for at in range(w_ref.shape[0] // 2):
            x = [keep_ref[0, at], far_ref[0, at], other_ref[0, at], far_ref[1, at]]
            part = dot(jnp.concatenate(x, axis=0), both_rows(w_ref, at))
            total = part if total is None else total + part
        for n, out_ref in enumerate(outs):
            out_ref[:, lane : lane + width] = total[n * rows : (n + 1) * rows]


def pack_kernel(query_ref, pair_ref, out_w_ref, out_ref, pair_buf, out_w_buf, split_buf, fold_buf, sems):
    rows = query_ref.shape[0]
    query = pltpu.make_async_copy(query_ref, out_ref.at[:rows], sems.at[0])
    pair = pltpu.make_async_copy(pair_ref, pair_buf, sems.at[1])
    out_w = pltpu.make_async_copy(out_w_ref, out_w_buf, sems.at[2])
    split = pltpu.make_async_copy(split_buf, out_ref.at[rows : 3 * rows], sems.at[3])
    fold = pltpu.make_async_copy(fold_buf, out_ref.at[3 * rows :], sems.at[4])
    pair.start()
    out_w.start()
    query.start()
    pair.wait()
    split_buf[:rows] = pair_buf[:, 0]
    split_buf[rows:] = pair_buf[:, 1]
    split.start()
    out_w.wait()
    fold_buf[...] = jnp.concatenate([out_w_buf[:rows], out_w_buf[rows:]], axis=1)
    fold.start()
    query.wait()
    split.wait()
    fold.wait()


def thirds(value):
    high = value.astype(jnp.bfloat16)
    rest = value - high.astype(jnp.float32)
    middle = rest.astype(jnp.bfloat16)
    low = (rest - middle.astype(jnp.float32)).astype(jnp.bfloat16)
    return [high.astype(jnp.float32), middle.astype(jnp.float32), low.astype(jnp.float32)]


def score(q, keys):
    return lax.dot_general(q, keys, (((1,), (1,)), ((), ())), preferred_element_type=jnp.float32)


def mixed(scores, peak, values):
    weights = jnp.exp2((scores - peak) * EXPONENT).astype(jnp.bfloat16)
    return dot(weights, jnp.concatenate([values, jnp.ones_like(values)], axis=1))


def cache_kernel(bias_ref, q_ref, k_ref, v_ref, peak_ref, total_ref, s_ref):
    q = q_ref[...]
    cache_rows = k_ref.shape[0]
    peak = None
    for at in range(0, cache_rows, KEY_ROWS):
        s = score(q, k_ref[at : at + KEY_ROWS]) + bias_ref[0:1, at : at + KEY_ROWS]
        s_ref[:, at : at + KEY_ROWS] = s
        for lane in range(0, KEY_ROWS, HD):
            piece = s[:, lane : lane + HD]
            peak = piece if peak is None else jnp.maximum(peak, piece)
    peak = jnp.max(peak, axis=1, keepdims=True)
    total = None
    for at in range(0, cache_rows, KEY_ROWS):
        part = mixed(s_ref[:, at : at + KEY_ROWS], peak, v_ref[at : at + KEY_ROWS])
        total = part if total is None else total + part
    peak_ref[0] = jnp.broadcast_to(peak, peak_ref.shape[1:])
    total_ref[0] = total


def new_kernel(place_ref, q_ref, *refs):
    *pair_refs, peak_ref, total_ref, out_ref = refs
    keys, values = [
        (near[...] + core[0] + far[...]).astype(jnp.bfloat16) for near, core, far in (pair_refs[:3], pair_refs[3:])
    ]
    s = score(q_ref[...], keys)
    row = pl.program_id(1) * QUERY_ROWS + lax.broadcasted_iota(jnp.int32, s.shape, 0)
    column = place_ref[2] * keys.shape[0] + lax.broadcasted_iota(jnp.int32, s.shape, 1)
    s = jnp.where(column <= row, s, DEAD)
    cache_peak = peak_ref[0]
    peak = jnp.maximum(cache_peak, jnp.max(s, axis=1, keepdims=True))
    fresh = mixed(s, peak, values)
    kept = jnp.exp2((cache_peak - peak) * EXPONENT)
    mixture = total_ref[0, :, :HD] * kept + fresh[:, :HD]
    total = total_ref[0, :, HD:] * kept + fresh[:, HD:]

    lane = lax.broadcasted_iota(jnp.int32, (HD, HD), 1)
    blocks, rows, _ = out_ref.shape
    own = rows - STAT_ROWS
    for b in range(blocks):
        part = slice(b * own, (b + 1) * own)
        out_ref[b, :own] = mixture[part].astype(jnp.bfloat16)
        turned = jnp.where(lane == 0, peak[part], total[part]).T
        stats = thirds(turned[0:1]) + thirds(turned[1:2])
        stats = jnp.concatenate([*stats, jnp.zeros((STAT_ROWS - 6, HD), jnp.float32)], axis=0)
        out_ref[b, own:] = stats.astype(jnp.bfloat16)


def finish_kernel(place_ref, parts_ref, w_ref, far_w_ref, swap_w_ref, swap_far_w_ref, out_ref):
    x_hi, core = place_ref[0], place_ref[1]
    sources, rows, width = parts_ref.shape
    own = rows - STAT_ROWS
    heads = []
    for at in range(0, width, HD):
        stats = [parts_ref[z, own:, at : at + HD].astype(jnp.float32) for z in range(sources)]
        peaks = [s[0:1] + s[1:2] + s[2:3] for s in stats]
        totals = [s[3:4] + s[4:5] + s[5:6] for s in stats]
        highest = peaks[0]
        for p in peaks[1:]:
            highest = jnp.maximum(highest, p)
        factors = [jnp.exp2((p - highest) * EXPONENT) for p in peaks]
        total = sum(f * t for f, t in zip(factors, totals))
        shares = [f / total for f in factors]
        shares = jnp.concatenate([*shares, jnp.zeros((HD - sources, HD), jnp.float32)], axis=0).T
        mixture = None
        for z in range(sources):
            part = parts_ref[z, :own, at : at + HD].astype(jnp.float32) * shares[:, z : z + 1]
            mixture = part if mixture is None else mixture + part
        heads.append(mixture.astype(jnp.bfloat16))
    attended = jnp.concatenate(heads, axis=1)
    lanes = w_ref.shape[1]
    sides = ((w_ref, x_hi, core), (far_w_ref, 1 - x_hi, core))
    sides += ((swap_w_ref, x_hi, 1 - core), (swap_far_w_ref, 1 - x_hi, 1 - core))
    for at in range(w_ref.shape[0]):
        lane = slice(at % 2 * lanes, (at % 2 + 1) * lanes)
        for ref, half, side in sides:
            w = jnp.concatenate([ref[at, :, :lanes], ref[at, :, lanes:]], axis=0)
            to = (2 * half + side) * 4 + at // 2
            out_ref[to, :, lane] = dot(attended, w).astype(jnp.bfloat16)


def in_hbm(value):
    return pltpu.with_memory_space_constraint(value, pltpu.HBM)


def doubled(value, axes):
    for axis in axes[:-1]:
        value = jnp.concatenate([value, swapped(value, axis)], axis=0)
    return value, swapped(value, axes[-1])


def shards(tokens, w_query, w_keyvalue, cache_keys, cache_values, key_start, key_end, w_out):
    local_rows, width = tokens.shape[1:]
    cache_rows = cache_keys.shape[1]
    kv = lax.axis_index(KV).astype(jnp.int32)
    kv_count = lax.axis_size(KV)
    own = jnp.stack([lax.axis_index("x_hi"), lax.axis_index("core"), kv]).astype(jnp.int32)

    def part_of_weights(index):
        block = (kv_count, local_rows, width)
        return pl.BlockSpec(block, lambda i: (0, index, 0)), in_hbm(weights)

    def call(kernel, shapes, *operands):
        pairs = [o if isinstance(o, tuple) else (WHOLE, o) for o in operands]
        return pl.pallas_call(
            kernel,
            grid=(1,),
            out_shape=shapes,
            in_specs=[SCALAR] + [spec for spec, _ in pairs],
            out_specs=jax.tree.map(lambda _: WHOLE, shapes),
            compiler_params=VMEM,
        )(own, *(operand for _, operand in pairs))

    gathered = shared(tokens[0], HEAD)
    query_w_far = swapped(w_query[None], "x_hi")
    query_w_far = doubled(query_w_far, KV)
    sources = [in_hbm(w) for w in (w_query, w_keyvalue, w_out)]
    weights = pl.pallas_call(
        pack_kernel,
        out_shape=jax.ShapeDtypeStruct((4 * local_rows, width), jnp.bfloat16),
        in_specs=[pl.BlockSpec(memory_space=pl.ANY)] * 3,
        out_specs=pl.BlockSpec(memory_space=pl.ANY),
        scratch_shapes=[
            pltpu.VMEM(w_keyvalue.shape, jnp.bfloat16),
            pltpu.VMEM(w_out.shape, jnp.bfloat16),
            pltpu.VMEM((2 * local_rows, width), jnp.bfloat16),
            pltpu.VMEM((local_rows, width), jnp.bfloat16),
            pltpu.SemaphoreType.DMA((5,)),
        ],
        name="pack",
    )(*sources)
    weights = lax.all_gather(weights, KV, axis=0, tiled=False)
    out_w = weights[:, 3 * local_rows :]
    out_w_far = swapped(out_w, "x_hi")
    out_w_core = swapped(out_w, "core")
    out_w_both = swapped(out_w_far, "core")

    half = jax.ShapeDtypeStruct((2, 4, local_rows, width), jnp.bfloat16)
    keep, send = call(normalize_kernel, (half, half), gathered)
    other = swapped(send, "core")
    partial = jax.ShapeDtypeStruct((local_rows, width), jnp.float32)
    mine, theirs = call(query_kernel, (partial, partial), keep, other, part_of_weights(0), *query_w_far)
    queries = (mine + swapped(theirs, "core")).astype(jnp.bfloat16)
    queries = shared(queries, KV).reshape(-1, width)

    far = swapped(jnp.stack([keep[1], other[1]]), "x_hi")
    partial = jax.ShapeDtypeStruct((local_rows, 2 * width), jnp.float32)
    both = jax.ShapeDtypeStruct((2, local_rows, 2 * width), jnp.float32)
    pair_near, pair_far, theirs = call(
        pair_kernel,
        (partial, partial, both),
        keep,
        other,
        far,
        part_of_weights(1),
        part_of_weights(2),
    )
    pair_core = swapped(theirs, "core")
    pair_far = swapped(pair_far + pair_core[1], "x_hi")
    place = kv * cache_rows + lax.iota(jnp.int32, cache_rows)
    usable = (place >= key_start[0]) & (place < key_end[0])
    bias = jnp.broadcast_to(jnp.where(usable, 0.0, DEAD).astype(jnp.float32)[None], (8, cache_rows))

    heads = width // HD
    rows = queries.shape[0]
    grid = (heads, rows // QUERY_ROWS)
    query_spec = pl.BlockSpec((QUERY_ROWS, HD), lambda h, i: (i, h))
    cache_spec = pl.BlockSpec((cache_rows, HD), lambda h, i: (0, h))
    peak_spec = pl.BlockSpec((1, QUERY_ROWS, HD), lambda h, i: (h, i, 0))
    total_spec = pl.BlockSpec((1, QUERY_ROWS, 2 * HD), lambda h, i: (h, i, 0))
    peaks, totals = pl.pallas_call(
        cache_kernel,
        grid=grid,
        out_shape=(
            jax.ShapeDtypeStruct((heads, rows, HD), jnp.float32),
            jax.ShapeDtypeStruct((heads, rows, 2 * HD), jnp.float32),
        ),
        in_specs=[pl.BlockSpec((8, cache_rows), lambda h, i: (0, 0)), query_spec, cache_spec, cache_spec],
        out_specs=(peak_spec, total_spec),
        scratch_shapes=[pltpu.VMEM((QUERY_ROWS, cache_rows), jnp.float32)],
        compiler_params=VMEM,
        name="attend_cache",
    )(bias, queries, in_hbm(cache_keys[0]), in_hbm(cache_values[0]))

    def pair_specs(first):
        flat = pl.BlockSpec((local_rows, HD), lambda h, i: (0, h + first))
        return flat, pl.BlockSpec((1, local_rows, HD), lambda h, i: (0, 0, h + first)), flat

    padded = local_rows + STAT_ROWS
    parts = pl.pallas_call(
        new_kernel,
        grid=grid,
        out_shape=jax.ShapeDtypeStruct((kv_count, padded, width), jnp.bfloat16),
        in_specs=[
            SCALAR,
            query_spec,
            *pair_specs(0),
            *pair_specs(heads),
            peak_spec,
            total_spec,
        ],
        out_specs=pl.BlockSpec((QUERY_ROWS // local_rows, padded, HD), lambda h, i: (i, 0, h)),
        compiler_params=VMEM,
        name="attend_new",
    )(own, queries, *(pair_near, pair_core, pair_far) * 2, peaks, totals)

    arrived = lax.all_to_all(parts, KV, split_axis=0, concat_axis=0, tiled=True)
    blocks = jax.ShapeDtypeStruct((lax.axis_size(HEAD), local_rows, width), jnp.bfloat16)
    columns = call(finish_kernel, blocks, arrived, out_w, out_w_far, out_w_core, out_w_both)
    columns = lax.all_to_all(columns, HEAD, split_axis=0, concat_axis=0, tiled=True)
    return columns.astype(jnp.float32).sum(axis=0).astype(jnp.bfloat16)[None]


def solution(mesh):
    section, head, kv = (mesh.shape[name] for name in ("section", "head", "kv"))
    torus = Mesh(
        mesh.devices.reshape(section // 2, 2, head // 2, 2, kv // 4, 2, 2),
        ("x_hi", "core", "y", "x_lo", *KV),
    )
    section = ("x_hi", "core")
    rows = (*section, *KV)
    return jax.shard_map(
        shards,
        mesh=torus,
        in_specs=(
            P(section, KV, HEAD),
            P(rows, HEAD),
            P(rows, None, HEAD),
            P(section, KV, HEAD),
            P(section, KV, HEAD),
            P(section),
            P(section),
            P(HEAD, rows),
        ),
        out_specs=P(section, KV, HEAD),
        check_vma=False,
    )
```

```python
import jax
import jax.numpy as jnp
from jax import lax
from jax.experimental import pallas as pl
from jax.experimental.pallas import tpu as pltpu
from jax.sharding import Mesh
from jax.sharding import PartitionSpec as P


HD = 128
HEAD = ("y", "x_lo")
KV = ("z_4", "z_2", "z_1")
STAT_ROWS = 16
QUERY_ROWS = 512
KEY_ROWS = 512
DEAD = -1e30
SCALE = HD**-0.5
EXPONENT = SCALE * 1.4426950408889634
VMEM = pltpu.CompilerParams(vmem_limit_bytes=48 * 1024 * 1024)
SCALAR = pl.BlockSpec(memory_space=pltpu.SMEM)
WHOLE = pl.BlockSpec(memory_space=pltpu.VMEM)
IN_PLACE = pl.BlockSpec(memory_space=pl.ANY)


def dot(a, b):
    return jnp.dot(a, b, preferred_element_type=jnp.float32)


def shared(value, axes):
    copies = jnp.broadcast_to(value, (lax.axis_size(axes), *value.shape))
    return lax.all_to_all(copies, axes, split_axis=0, concat_axis=0, tiled=True)


def swapped(value, axis):
    return lax.ppermute(value, axis, [(0, 1), (1, 0)])


def normalize_kernel(place_ref, x_ref, keep_ref, send_ref):
    x_hi, core = place_ref[0], place_ref[1]
    blocks = x_ref.shape[0]
    squares = None
    for b in range(blocks):
        x = x_ref[b].astype(jnp.float32)
        squares = x * x if squares is None else squares + x * x
    mean = jnp.sum(squares, axis=1, keepdims=True) / (blocks * x_ref.shape[2])
    factor = lax.rsqrt(mean + 1e-05)
    for far in range(2):
        half = 1 - x_hi if far else x_hi
        for j in range(4):
            for out_ref, side in ((keep_ref, core), (send_ref, 1 - core)):
                x = x_ref[half * 8 + side * 4 + j].astype(jnp.float32)
                out_ref[far, j] = (x * factor).astype(jnp.bfloat16)


def both_rows(w_ref, at):
    return jnp.concatenate([w_ref[2 * at], w_ref[2 * at + 1]], axis=0)


def query_kernel(place_ref, keep_ref, other_ref, w_ref, far_w_ref, away_w_ref, own_out, other_out):
    kv = place_ref[2]
    lanes = far_w_ref.shape[1]
    near = pl.multiple_of((kv & 1) * lanes, lanes)
    away = pl.multiple_of((1 - (kv & 1)) * lanes, lanes)
    total = None
    for at in range(w_ref.shape[0] // 2):
        x = jnp.concatenate([keep_ref[0, at], other_ref[0, at]], axis=0)
        part = dot(x, both_rows(w_ref, at))
        total = part if total is None else total + part
    for at in range(far_w_ref.shape[0]):
        flip_4, flip_2 = at % 2, at // 2
        rows = (kv >> 1) ^ (2 * flip_4 + flip_2)
        for ref, lane in ((far_w_ref, near), (away_w_ref, away)):
            x = [tile[1, rows, :, pl.ds(lane, lanes)] for tile in (keep_ref, other_ref)]
            total = total + dot(jnp.concatenate(x, axis=0), ref[at])
    own_out[...] = total[: own_out.shape[0]]
    other_out[...] = total[own_out.shape[0] :]


def pair_kernel(place_ref, keep_ref, other_ref, far_ref, key_w_ref, value_w_ref, packed_ref, *refs):
    near_out, far_out, other_out, out_w_ref, sem = refs
    last = packed_ref.shape[1] - out_w_ref.shape[1]
    out_w = pltpu.make_async_copy(packed_ref.at[:, last:], out_w_ref, sem)
    out_w.start()
    rows, width = near_out.shape[0], key_w_ref.shape[2]
    outs = (near_out, far_out, other_out.at[0], other_out.at[1])
    for lane, w_ref in ((0, key_w_ref), (width, value_w_ref)):
        total = None
        for at in range(w_ref.shape[0] // 2):
            x = [keep_ref[0, at], far_ref[0, at], other_ref[0, at], far_ref[1, at]]
            part = dot(jnp.concatenate(x, axis=0), both_rows(w_ref, at))
            total = part if total is None else total + part
        for n, out_ref in enumerate(outs):
            out_ref[:, lane : lane + width] = total[n * rows : (n + 1) * rows]
    out_w.wait()


def pack_kernel(query_ref, pair_ref, out_w_ref, out_ref, pair_buf, out_w_buf, split_buf, fold_buf, sems):
    rows = query_ref.shape[0]
    query = pltpu.make_async_copy(query_ref, out_ref.at[:rows], sems.at[0])
    pair = pltpu.make_async_copy(pair_ref, pair_buf, sems.at[1])
    out_w = pltpu.make_async_copy(out_w_ref, out_w_buf, sems.at[2])
    split = pltpu.make_async_copy(split_buf, out_ref.at[rows : 3 * rows], sems.at[3])
    fold = pltpu.make_async_copy(fold_buf, out_ref.at[3 * rows :], sems.at[4])
    pair.start()
    out_w.start()
    query.start()
    pair.wait()
    split_buf[:rows] = pair_buf[:, 0]
    split_buf[rows:] = pair_buf[:, 1]
    split.start()
    out_w.wait()
    fold_buf[...] = jnp.concatenate([out_w_buf[:rows], out_w_buf[rows:]], axis=1)
    fold.start()
    query.wait()
    split.wait()
    fold.wait()


def thirds(value):
    high = value.astype(jnp.bfloat16)
    rest = value - high.astype(jnp.float32)
    middle = rest.astype(jnp.bfloat16)
    low = (rest - middle.astype(jnp.float32)).astype(jnp.bfloat16)
    return [high.astype(jnp.float32), middle.astype(jnp.float32), low.astype(jnp.float32)]


def score(q, keys):
    return lax.dot_general(q, keys, (((1,), (1,)), ((), ())), preferred_element_type=jnp.float32)


def mixed(scores, peak, values):
    weights = jnp.exp2((scores - peak) * EXPONENT).astype(jnp.bfloat16)
    return dot(weights, jnp.concatenate([values, jnp.ones_like(values)], axis=1))


def cache_kernel(bias_ref, q_ref, k_ref, v_ref, peak_ref, total_ref, s_ref):
    q = q_ref[...]
    cache_rows = k_ref.shape[0]
    peak = None
    for at in range(0, cache_rows, KEY_ROWS):
        s = score(q, k_ref[at : at + KEY_ROWS]) + bias_ref[0:1, at : at + KEY_ROWS]
        s_ref[:, at : at + KEY_ROWS] = s
        for lane in range(0, KEY_ROWS, HD):
            piece = s[:, lane : lane + HD]
            peak = piece if peak is None else jnp.maximum(peak, piece)
    peak = jnp.max(peak, axis=1, keepdims=True)
    total = None
    for at in range(0, cache_rows, KEY_ROWS):
        part = mixed(s_ref[:, at : at + KEY_ROWS], peak, v_ref[at : at + KEY_ROWS])
        total = part if total is None else total + part
    peak_ref[0] = jnp.broadcast_to(peak, peak_ref.shape[1:])
    total_ref[0] = total


def new_kernel(place_ref, q_ref, *refs):
    *pair_refs, peak_ref, total_ref, out_ref = refs
    keys, values = [
        (near[...] + core[0] + far[...]).astype(jnp.bfloat16) for near, core, far in (pair_refs[:3], pair_refs[3:])
    ]
    s = score(q_ref[...], keys)
    row = pl.program_id(1) * QUERY_ROWS + lax.broadcasted_iota(jnp.int32, s.shape, 0)
    column = place_ref[2] * keys.shape[0] + lax.broadcasted_iota(jnp.int32, s.shape, 1)
    s = jnp.where(column <= row, s, DEAD)
    cache_peak = peak_ref[0]
    peak = jnp.maximum(cache_peak, jnp.max(s, axis=1, keepdims=True))
    fresh = mixed(s, peak, values)
    kept = jnp.exp2((cache_peak - peak) * EXPONENT)
    mixture = total_ref[0, :, :HD] * kept + fresh[:, :HD]
    total = total_ref[0, :, HD:] * kept + fresh[:, HD:]

    lane = lax.broadcasted_iota(jnp.int32, (HD, HD), 1)
    blocks, rows, _ = out_ref.shape
    own = rows - STAT_ROWS
    for b in range(blocks):
        part = slice(b * own, (b + 1) * own)
        out_ref[b, :own] = mixture[part].astype(jnp.bfloat16)
        turned = jnp.where(lane == 0, peak[part], total[part]).T
        stats = thirds(turned[0:1]) + thirds(turned[1:2])
        stats = jnp.concatenate([*stats, jnp.zeros((STAT_ROWS - 6, HD), jnp.float32)], axis=0)
        out_ref[b, own:] = stats.astype(jnp.bfloat16)


def finish_kernel(place_ref, parts_ref, w_ref, far_w_ref, swap_w_ref, swap_far_w_ref, out_ref):
    x_hi, core = place_ref[0], place_ref[1]
    sources, rows, width = parts_ref.shape
    own = rows - STAT_ROWS
    heads = []
    for at in range(0, width, HD):
        stats = [parts_ref[z, own:, at : at + HD].astype(jnp.float32) for z in range(sources)]
        peaks = [s[0:1] + s[1:2] + s[2:3] for s in stats]
        totals = [s[3:4] + s[4:5] + s[5:6] for s in stats]
        highest = peaks[0]
        for p in peaks[1:]:
            highest = jnp.maximum(highest, p)
        factors = [jnp.exp2((p - highest) * EXPONENT) for p in peaks]
        total = sum(f * t for f, t in zip(factors, totals))
        shares = [f / total for f in factors]
        shares = jnp.concatenate([*shares, jnp.zeros((HD - sources, HD), jnp.float32)], axis=0).T
        mixture = None
        for z in range(sources):
            part = parts_ref[z, :own, at : at + HD].astype(jnp.float32) * shares[:, z : z + 1]
            mixture = part if mixture is None else mixture + part
        heads.append(mixture.astype(jnp.bfloat16))
    attended = jnp.concatenate(heads, axis=1)
    lanes = w_ref.shape[1]
    sides = ((w_ref, x_hi, core), (far_w_ref, 1 - x_hi, core))
    sides += ((swap_w_ref, x_hi, 1 - core), (swap_far_w_ref, 1 - x_hi, 1 - core))
    for at in range(w_ref.shape[0]):
        lane = slice(at % 2 * lanes, (at % 2 + 1) * lanes)
        for ref, half, side in sides:
            w = jnp.concatenate([ref[at, :, :lanes], ref[at, :, lanes:]], axis=0)
            to = (2 * half + side) * 4 + at // 2
            out_ref[to, :, lane] = dot(attended, w).astype(jnp.bfloat16)


def in_hbm(value):
    return pltpu.with_memory_space_constraint(value, pltpu.HBM)


def doubled(value, axes):
    for axis in axes[:-1]:
        value = jnp.concatenate([value, swapped(value, axis)], axis=0)
    return value, swapped(value, axes[-1])


def shards(tokens, w_query, w_keyvalue, cache_keys, cache_values, key_start, key_end, w_out):
    local_rows, width = tokens.shape[1:]
    cache_rows = cache_keys.shape[1]
    kv = lax.axis_index(KV).astype(jnp.int32)
    kv_count = lax.axis_size(KV)
    own = jnp.stack([lax.axis_index("x_hi"), lax.axis_index("core"), kv]).astype(jnp.int32)

    def part_of_weights(index):
        block = (kv_count, local_rows, width)
        return pl.BlockSpec(block, lambda i: (0, index, 0)), in_hbm(weights)

    def call(kernel, shapes, *operands, out_specs=None, scratch=()):
        pairs = [o if isinstance(o, tuple) else (WHOLE, o) for o in operands]
        return pl.pallas_call(
            kernel,
            grid=(1,),
            out_shape=shapes,
            in_specs=[SCALAR] + [spec for spec, _ in pairs],
            out_specs=out_specs or jax.tree.map(lambda _: WHOLE, shapes),
            scratch_shapes=scratch,
            compiler_params=VMEM,
        )(own, *(operand for _, operand in pairs))

    gathered = shared(tokens[0], HEAD)
    query_w_far = swapped(w_query[None], "x_hi")
    query_w_far = doubled(query_w_far, KV)
    sources = [in_hbm(w) for w in (w_query, w_keyvalue, w_out)]
    weights = pl.pallas_call(
        pack_kernel,
        out_shape=jax.ShapeDtypeStruct((4 * local_rows, width), jnp.bfloat16),
        in_specs=[pl.BlockSpec(memory_space=pl.ANY)] * 3,
        out_specs=pl.BlockSpec(memory_space=pl.ANY),
        scratch_shapes=[
            pltpu.VMEM(w_keyvalue.shape, jnp.bfloat16),
            pltpu.VMEM(w_out.shape, jnp.bfloat16),
            pltpu.VMEM((2 * local_rows, width), jnp.bfloat16),
            pltpu.VMEM((local_rows, width), jnp.bfloat16),
            pltpu.SemaphoreType.DMA((5,)),
        ],
        name="pack",
    )(*sources)
    weights = lax.all_gather(weights, KV, axis=0, tiled=False)

    half = jax.ShapeDtypeStruct((2, 4, local_rows, width), jnp.bfloat16)
    keep, send = call(normalize_kernel, (half, half), gathered)
    other = swapped(send, "core")
    partial = jax.ShapeDtypeStruct((local_rows, width), jnp.float32)
    mine, theirs = call(query_kernel, (partial, partial), keep, other, part_of_weights(0), *query_w_far)
    queries = (mine + swapped(theirs, "core")).astype(jnp.bfloat16)
    queries = shared(queries, KV).reshape(-1, width)

    far = swapped(jnp.stack([keep[1], other[1]]), "x_hi")
    partial = jax.ShapeDtypeStruct((local_rows, 2 * width), jnp.float32)
    both = jax.ShapeDtypeStruct((2, local_rows, 2 * width), jnp.float32)
    pair_near, pair_far, theirs, out_w = call(
        pair_kernel,
        (partial, partial, both, jax.ShapeDtypeStruct((kv_count, local_rows, width), jnp.bfloat16)),
        keep,
        other,
        far,
        part_of_weights(1),
        part_of_weights(2),
        (IN_PLACE, in_hbm(weights)),
        out_specs=(WHOLE, WHOLE, WHOLE, IN_PLACE),
        scratch=[pltpu.SemaphoreType.DMA],
    )
    pair_core = swapped(theirs, "core")
    pair_far = swapped(pair_far + pair_core[1], "x_hi")
    out_w_far = swapped(out_w, "x_hi")
    out_w_core = swapped(out_w, "core")
    out_w_both = swapped(out_w_far, "core")

    place = kv * cache_rows + lax.iota(jnp.int32, cache_rows)
    usable = (place >= key_start[0]) & (place < key_end[0])
    bias = jnp.broadcast_to(jnp.where(usable, 0.0, DEAD).astype(jnp.float32)[None], (8, cache_rows))

    heads = width // HD
    rows = queries.shape[0]
    grid = (heads, rows // QUERY_ROWS)
    query_spec = pl.BlockSpec((QUERY_ROWS, HD), lambda h, i: (i, h))
    cache_spec = pl.BlockSpec((cache_rows, HD), lambda h, i: (0, h))
    peak_spec = pl.BlockSpec((1, QUERY_ROWS, HD), lambda h, i: (h, i, 0))
    total_spec = pl.BlockSpec((1, QUERY_ROWS, 2 * HD), lambda h, i: (h, i, 0))
    peaks, totals = pl.pallas_call(
        cache_kernel,
        grid=grid,
        out_shape=(
            jax.ShapeDtypeStruct((heads, rows, HD), jnp.float32),
            jax.ShapeDtypeStruct((heads, rows, 2 * HD), jnp.float32),
        ),
        in_specs=[pl.BlockSpec((8, cache_rows), lambda h, i: (0, 0)), query_spec, cache_spec, cache_spec],
        out_specs=(peak_spec, total_spec),
        scratch_shapes=[pltpu.VMEM((QUERY_ROWS, cache_rows), jnp.float32)],
        compiler_params=VMEM,
        name="attend_cache",
    )(bias, queries, in_hbm(cache_keys[0]), in_hbm(cache_values[0]))

    def pair_specs(first):
        flat = pl.BlockSpec((local_rows, HD), lambda h, i: (0, h + first))
        return flat, pl.BlockSpec((1, local_rows, HD), lambda h, i: (0, 0, h + first)), flat

    padded = local_rows + STAT_ROWS
    parts = pl.pallas_call(
        new_kernel,
        grid=grid,
        out_shape=jax.ShapeDtypeStruct((kv_count, padded, width), jnp.bfloat16),
        in_specs=[
            SCALAR,
            query_spec,
            *pair_specs(0),
            *pair_specs(heads),
            peak_spec,
            total_spec,
        ],
        out_specs=pl.BlockSpec((QUERY_ROWS // local_rows, padded, HD), lambda h, i: (i, 0, h)),
        compiler_params=VMEM,
        name="attend_new",
    )(own, queries, *(pair_near, pair_core, pair_far) * 2, peaks, totals)

    arrived = lax.all_to_all(parts, KV, split_axis=0, concat_axis=0, tiled=True)
    blocks = jax.ShapeDtypeStruct((lax.axis_size(HEAD), local_rows, width), jnp.bfloat16)
    columns = call(finish_kernel, blocks, arrived, out_w, out_w_far, out_w_core, out_w_both)
    columns = lax.all_to_all(columns, HEAD, split_axis=0, concat_axis=0, tiled=True)
    return columns.astype(jnp.float32).sum(axis=0).astype(jnp.bfloat16)[None]


def solution(mesh):
    section, head, kv = (mesh.shape[name] for name in ("section", "head", "kv"))
    torus = Mesh(
        mesh.devices.reshape(section // 2, 2, head // 2, 2, kv // 4, 2, 2),
        ("x_hi", "core", "y", "x_lo", *KV),
    )
    section = ("x_hi", "core")
    rows = (*section, *KV)
    return jax.shard_map(
        shards,
        mesh=torus,
        in_specs=(
            P(section, KV, HEAD),
            P(rows, HEAD),
            P(rows, None, HEAD),
            P(section, KV, HEAD),
            P(section, KV, HEAD),
            P(section),
            P(section),
            P(HEAD, rows),
        ),
        out_specs=P(section, KV, HEAD),
        check_vma=False,
    )
```

```python
import jax
import jax.numpy as jnp
from jax import lax
from jax.experimental import pallas as pl
from jax.experimental.pallas import tpu as pltpu
from jax.sharding import Mesh
from jax.sharding import PartitionSpec as P


HD = 128
HEAD = ("y", "x_lo")
KV = ("z_4", "z_2", "z_1")
STAT_ROWS = 16
QUERY_ROWS = 512
NEW_ROWS = 1024
KEY_ROWS = 512
DEAD = -1e30
SCALE = HD**-0.5
EXPONENT = SCALE * 1.4426950408889634
VMEM = pltpu.CompilerParams(vmem_limit_bytes=48 * 1024 * 1024)
SCALAR = pl.BlockSpec(memory_space=pltpu.SMEM)
WHOLE = pl.BlockSpec(memory_space=pltpu.VMEM)
IN_PLACE = pl.BlockSpec(memory_space=pl.ANY)


def dot(a, b):
    return jnp.dot(a, b, preferred_element_type=jnp.float32)


def shared(value, axes):
    copies = jnp.broadcast_to(value, (lax.axis_size(axes), *value.shape))
    return lax.all_to_all(copies, axes, split_axis=0, concat_axis=0, tiled=True)


def swapped(value, axis):
    return lax.ppermute(value, axis, [(0, 1), (1, 0)])


def normalize_kernel(place_ref, x_ref, keep_ref, send_ref):
    x_hi, core = place_ref[0], place_ref[1]
    blocks = x_ref.shape[0]
    squares = None
    for b in range(blocks):
        x = x_ref[b].astype(jnp.float32)
        squares = x * x if squares is None else squares + x * x
    mean = jnp.sum(squares, axis=1, keepdims=True) / (blocks * x_ref.shape[2])
    factor = lax.rsqrt(mean + 1e-05)
    for far in range(2):
        half = 1 - x_hi if far else x_hi
        for j in range(4):
            for out_ref, side in ((keep_ref, core), (send_ref, 1 - core)):
                x = x_ref[half * 8 + side * 4 + j].astype(jnp.float32)
                out_ref[far, j] = (x * factor).astype(jnp.bfloat16)


def both_rows(w_ref, at):
    return jnp.concatenate([w_ref[2 * at], w_ref[2 * at + 1]], axis=0)


def query_kernel(place_ref, keep_ref, other_ref, w_ref, far_w_ref, away_w_ref, own_out, other_out):
    kv = place_ref[2]
    lanes = far_w_ref.shape[1]
    near = pl.multiple_of((kv & 1) * lanes, lanes)
    away = pl.multiple_of((1 - (kv & 1)) * lanes, lanes)
    total = None
    for at in range(w_ref.shape[0] // 2):
        x = jnp.concatenate([keep_ref[0, at], other_ref[0, at]], axis=0)
        part = dot(x, both_rows(w_ref, at))
        total = part if total is None else total + part
    for at in range(far_w_ref.shape[0]):
        flip_4, flip_2 = at % 2, at // 2
        rows = (kv >> 1) ^ (2 * flip_4 + flip_2)
        for ref, lane in ((far_w_ref, near), (away_w_ref, away)):
            x = [tile[1, rows, :, pl.ds(lane, lanes)] for tile in (keep_ref, other_ref)]
            total = total + dot(jnp.concatenate(x, axis=0), ref[at])
    own_out[...] = total[: own_out.shape[0]]
    other_out[...] = total[own_out.shape[0] :]


def pair_kernel(place_ref, keep_ref, other_ref, far_ref, key_w_ref, value_w_ref, packed_ref, *refs):
    near_out, far_out, other_out, out_w_ref, sem = refs
    last = packed_ref.shape[1] - out_w_ref.shape[1]
    out_w = pltpu.make_async_copy(packed_ref.at[:, last:], out_w_ref, sem)
    out_w.start()
    rows, width = near_out.shape[0], key_w_ref.shape[2]
    outs = (near_out, far_out, other_out.at[0], other_out.at[1])
    for lane, w_ref in ((0, key_w_ref), (width, value_w_ref)):
        total = None
        for at in range(w_ref.shape[0] // 2):
            x = [keep_ref[0, at], far_ref[0, at], other_ref[0, at], far_ref[1, at]]
            part = dot(jnp.concatenate(x, axis=0), both_rows(w_ref, at))
            total = part if total is None else total + part
        for n, out_ref in enumerate(outs):
            out_ref[:, lane : lane + width] = total[n * rows : (n + 1) * rows]
    out_w.wait()


def pack_kernel(query_ref, pair_ref, out_w_ref, out_ref, pair_buf, out_w_buf, split_buf, fold_buf, sems):
    rows = query_ref.shape[0]
    query = pltpu.make_async_copy(query_ref, out_ref.at[:rows], sems.at[0])
    pair = pltpu.make_async_copy(pair_ref, pair_buf, sems.at[1])
    out_w = pltpu.make_async_copy(out_w_ref, out_w_buf, sems.at[2])
    split = pltpu.make_async_copy(split_buf, out_ref.at[rows : 3 * rows], sems.at[3])
    fold = pltpu.make_async_copy(fold_buf, out_ref.at[3 * rows :], sems.at[4])
    pair.start()
    out_w.start()
    query.start()
    pair.wait()
    split_buf[:rows] = pair_buf[:, 0]
    split_buf[rows:] = pair_buf[:, 1]
    split.start()
    out_w.wait()
    fold_buf[...] = jnp.concatenate([out_w_buf[:rows], out_w_buf[rows:]], axis=1)
    fold.start()
    query.wait()
    split.wait()
    fold.wait()


def thirds(value):
    high = value.astype(jnp.bfloat16)
    rest = value - high.astype(jnp.float32)
    middle = rest.astype(jnp.bfloat16)
    low = (rest - middle.astype(jnp.float32)).astype(jnp.bfloat16)
    return [high.astype(jnp.float32), middle.astype(jnp.float32), low.astype(jnp.float32)]


def score(q, keys):
    return lax.dot_general(q, keys, (((1,), (1,)), ((), ())), preferred_element_type=jnp.float32)


def mixed(scores, peak, values):
    weights = jnp.exp2((scores - peak) * EXPONENT).astype(jnp.bfloat16)
    return dot(weights, jnp.concatenate([values, jnp.ones_like(values)], axis=1))


def cache_kernel(bias_ref, q_ref, k_ref, v_ref, peak_ref, total_ref, s_ref):
    q = q_ref[...]
    cache_rows = k_ref.shape[0]
    peak = None
    for at in range(0, cache_rows, KEY_ROWS):
        s = score(q, k_ref[at : at + KEY_ROWS]) + bias_ref[0:1, at : at + KEY_ROWS]
        s_ref[:, at : at + KEY_ROWS] = s
        for lane in range(0, KEY_ROWS, HD):
            piece = s[:, lane : lane + HD]
            peak = piece if peak is None else jnp.maximum(peak, piece)
    peak = jnp.max(peak, axis=1, keepdims=True)
    total = None
    for at in range(0, cache_rows, KEY_ROWS):
        part = mixed(s_ref[:, at : at + KEY_ROWS], peak, v_ref[at : at + KEY_ROWS])
        total = part if total is None else total + part
    peak_ref[0] = jnp.broadcast_to(peak, peak_ref.shape[1:])
    total_ref[0] = total


def new_kernel(place_ref, q_ref, *refs):
    *pair_refs, peak_ref, total_ref, out_ref = refs
    keys, values = [
        (near[...] + core[0] + far[...]).astype(jnp.bfloat16) for near, core, far in (pair_refs[:3], pair_refs[3:])
    ]
    s = score(q_ref[...], keys)
    row = pl.program_id(1) * NEW_ROWS + lax.broadcasted_iota(jnp.int32, s.shape, 0)
    column = place_ref[2] * keys.shape[0] + lax.broadcasted_iota(jnp.int32, s.shape, 1)
    s = jnp.where(column <= row, s, DEAD)
    cache_peak = peak_ref[0]
    peak = jnp.maximum(cache_peak, jnp.max(s, axis=1, keepdims=True))
    fresh = mixed(s, peak, values)
    kept = jnp.exp2((cache_peak - peak) * EXPONENT)
    mixture = total_ref[0, :, :HD] * kept + fresh[:, :HD]
    total = total_ref[0, :, HD:] * kept + fresh[:, HD:]

    lane = lax.broadcasted_iota(jnp.int32, (HD, HD), 1)
    blocks, rows, _ = out_ref.shape
    own = rows - STAT_ROWS
    for b in range(blocks):
        part = slice(b * own, (b + 1) * own)
        out_ref[b, :own] = mixture[part].astype(jnp.bfloat16)
        turned = jnp.where(lane == 0, peak[part], total[part]).T
        stats = thirds(turned[0:1]) + thirds(turned[1:2])
        stats = jnp.concatenate([*stats, jnp.zeros((STAT_ROWS - 6, HD), jnp.float32)], axis=0)
        out_ref[b, own:] = stats.astype(jnp.bfloat16)


def finish_kernel(place_ref, parts_ref, w_ref, far_w_ref, swap_w_ref, swap_far_w_ref, out_ref):
    x_hi, core = place_ref[0], place_ref[1]
    sources, rows, width = parts_ref.shape
    own = rows - STAT_ROWS
    heads = []
    for at in range(0, width, HD):
        stats = [parts_ref[z, own:, at : at + HD].astype(jnp.float32) for z in range(sources)]
        peaks = [s[0:1] + s[1:2] + s[2:3] for s in stats]
        totals = [s[3:4] + s[4:5] + s[5:6] for s in stats]
        highest = peaks[0]
        for p in peaks[1:]:
            highest = jnp.maximum(highest, p)
        factors = [jnp.exp2((p - highest) * EXPONENT) for p in peaks]
        total = sum(f * t for f, t in zip(factors, totals))
        shares = [f / total for f in factors]
        shares = jnp.concatenate([*shares, jnp.zeros((HD - sources, HD), jnp.float32)], axis=0).T
        mixture = None
        for z in range(sources):
            part = parts_ref[z, :own, at : at + HD].astype(jnp.float32) * shares[:, z : z + 1]
            mixture = part if mixture is None else mixture + part
        heads.append(mixture.astype(jnp.bfloat16))
    attended = jnp.concatenate(heads, axis=1)
    lanes = w_ref.shape[1]
    sides = ((w_ref, x_hi, core), (far_w_ref, 1 - x_hi, core))
    sides += ((swap_w_ref, x_hi, 1 - core), (swap_far_w_ref, 1 - x_hi, 1 - core))
    for at in range(w_ref.shape[0]):
        lane = slice(at % 2 * lanes, (at % 2 + 1) * lanes)
        for ref, half, side in sides:
            w = jnp.concatenate([ref[at, :, :lanes], ref[at, :, lanes:]], axis=0)
            to = (2 * half + side) * 4 + at // 2
            out_ref[to, :, lane] = dot(attended, w).astype(jnp.bfloat16)


def in_hbm(value):
    return pltpu.with_memory_space_constraint(value, pltpu.HBM)


def doubled(value, axes):
    for axis in axes[:-1]:
        value = jnp.concatenate([value, swapped(value, axis)], axis=0)
    return value, swapped(value, axes[-1])


def shards(tokens, w_query, w_keyvalue, cache_keys, cache_values, key_start, key_end, w_out):
    local_rows, width = tokens.shape[1:]
    cache_rows = cache_keys.shape[1]
    kv = lax.axis_index(KV).astype(jnp.int32)
    kv_count = lax.axis_size(KV)
    own = jnp.stack([lax.axis_index("x_hi"), lax.axis_index("core"), kv]).astype(jnp.int32)

    def part_of_weights(index):
        block = (kv_count, local_rows, width)
        return pl.BlockSpec(block, lambda i: (0, index, 0)), in_hbm(weights)

    def call(kernel, shapes, *operands, out_specs=None, scratch=()):
        pairs = [o if isinstance(o, tuple) else (WHOLE, o) for o in operands]
        return pl.pallas_call(
            kernel,
            grid=(1,),
            out_shape=shapes,
            in_specs=[SCALAR] + [spec for spec, _ in pairs],
            out_specs=out_specs or jax.tree.map(lambda _: WHOLE, shapes),
            scratch_shapes=scratch,
            compiler_params=VMEM,
        )(own, *(operand for _, operand in pairs))

    gathered = shared(tokens[0], HEAD)
    query_w_far = swapped(w_query[None], "x_hi")
    query_w_far = doubled(query_w_far, KV)
    sources = [in_hbm(w) for w in (w_query, w_keyvalue, w_out)]
    weights = pl.pallas_call(
        pack_kernel,
        out_shape=jax.ShapeDtypeStruct((4 * local_rows, width), jnp.bfloat16),
        in_specs=[pl.BlockSpec(memory_space=pl.ANY)] * 3,
        out_specs=pl.BlockSpec(memory_space=pl.ANY),
        scratch_shapes=[
            pltpu.VMEM(w_keyvalue.shape, jnp.bfloat16),
            pltpu.VMEM(w_out.shape, jnp.bfloat16),
            pltpu.VMEM((2 * local_rows, width), jnp.bfloat16),
            pltpu.VMEM((local_rows, width), jnp.bfloat16),
            pltpu.SemaphoreType.DMA((5,)),
        ],
        name="pack",
    )(*sources)
    weights = lax.all_gather(weights, KV, axis=0, tiled=False)

    half = jax.ShapeDtypeStruct((2, 4, local_rows, width), jnp.bfloat16)
    keep, send = call(normalize_kernel, (half, half), gathered)
    other = swapped(send, "core")
    partial = jax.ShapeDtypeStruct((local_rows, width), jnp.float32)
    mine, theirs = call(query_kernel, (partial, partial), keep, other, part_of_weights(0), *query_w_far)
    queries = (mine + swapped(theirs, "core")).astype(jnp.bfloat16)
    queries = shared(queries, KV).reshape(-1, width)

    far = swapped(jnp.stack([keep[1], other[1]]), "x_hi")
    partial = jax.ShapeDtypeStruct((local_rows, 2 * width), jnp.float32)
    both = jax.ShapeDtypeStruct((2, local_rows, 2 * width), jnp.float32)
    pair_near, pair_far, theirs, out_w = call(
        pair_kernel,
        (partial, partial, both, jax.ShapeDtypeStruct((kv_count, local_rows, width), jnp.bfloat16)),
        keep,
        other,
        far,
        part_of_weights(1),
        part_of_weights(2),
        (IN_PLACE, in_hbm(weights)),
        out_specs=(WHOLE, WHOLE, WHOLE, IN_PLACE),
        scratch=[pltpu.SemaphoreType.DMA],
    )
    pair_core = swapped(theirs, "core")
    pair_far = swapped(pair_far + pair_core[1], "x_hi")
    out_w_far = swapped(out_w, "x_hi")
    out_w_core = swapped(out_w, "core")
    out_w_both = swapped(out_w_far, "core")

    place = kv * cache_rows + lax.iota(jnp.int32, cache_rows)
    usable = (place >= key_start[0]) & (place < key_end[0])
    bias = jnp.broadcast_to(jnp.where(usable, 0.0, DEAD).astype(jnp.float32)[None], (8, cache_rows))

    heads = width // HD
    rows = queries.shape[0]
    grid = (heads, rows // QUERY_ROWS)
    query_spec = pl.BlockSpec((QUERY_ROWS, HD), lambda h, i: (i, h))
    cache_spec = pl.BlockSpec((cache_rows, HD), lambda h, i: (0, h))
    peak_spec = pl.BlockSpec((1, QUERY_ROWS, HD), lambda h, i: (h, i, 0))
    total_spec = pl.BlockSpec((1, QUERY_ROWS, 2 * HD), lambda h, i: (h, i, 0))
    peaks, totals = pl.pallas_call(
        cache_kernel,
        grid=grid,
        out_shape=(
            jax.ShapeDtypeStruct((heads, rows, HD), jnp.float32),
            jax.ShapeDtypeStruct((heads, rows, 2 * HD), jnp.float32),
        ),
        in_specs=[pl.BlockSpec((8, cache_rows), lambda h, i: (0, 0)), query_spec, cache_spec, cache_spec],
        out_specs=(peak_spec, total_spec),
        scratch_shapes=[pltpu.VMEM((QUERY_ROWS, cache_rows), jnp.float32)],
        compiler_params=VMEM,
        name="attend_cache",
    )(bias, queries, in_hbm(cache_keys[0]), in_hbm(cache_values[0]))

    def pair_specs(first):
        flat = pl.BlockSpec((local_rows, HD), lambda h, i: (0, h + first))
        return flat, pl.BlockSpec((1, local_rows, HD), lambda h, i: (0, 0, h + first)), flat

    padded = local_rows + STAT_ROWS
    parts = pl.pallas_call(
        new_kernel,
        grid=(heads, rows // NEW_ROWS),
        out_shape=jax.ShapeDtypeStruct((kv_count, padded, width), jnp.bfloat16),
        in_specs=[
            SCALAR,
            pl.BlockSpec((NEW_ROWS, HD), lambda h, i: (i, h)),
            *pair_specs(0),
            *pair_specs(heads),
            pl.BlockSpec((1, NEW_ROWS, HD), lambda h, i: (h, i, 0)),
            pl.BlockSpec((1, NEW_ROWS, 2 * HD), lambda h, i: (h, i, 0)),
        ],
        out_specs=pl.BlockSpec((NEW_ROWS // local_rows, padded, HD), lambda h, i: (i, 0, h)),
        compiler_params=VMEM,
        name="attend_new",
    )(own, queries, *(pair_near, pair_core, pair_far) * 2, peaks, totals)

    arrived = lax.all_to_all(parts, KV, split_axis=0, concat_axis=0, tiled=True)
    blocks = jax.ShapeDtypeStruct((lax.axis_size(HEAD), local_rows, width), jnp.bfloat16)
    columns = call(finish_kernel, blocks, arrived, out_w, out_w_far, out_w_core, out_w_both)
    columns = lax.all_to_all(columns, HEAD, split_axis=0, concat_axis=0, tiled=True)
    return columns.astype(jnp.float32).sum(axis=0).astype(jnp.bfloat16)[None]


def solution(mesh):
    section, head, kv = (mesh.shape[name] for name in ("section", "head", "kv"))
    torus = Mesh(
        mesh.devices.reshape(section // 2, 2, head // 2, 2, kv // 4, 2, 2),
        ("x_hi", "core", "y", "x_lo", *KV),
    )
    section = ("x_hi", "core")
    rows = (*section, *KV)
    return jax.shard_map(
        shards,
        mesh=torus,
        in_specs=(
            P(section, KV, HEAD),
            P(rows, HEAD),
            P(rows, None, HEAD),
            P(section, KV, HEAD),
            P(section, KV, HEAD),
            P(section),
            P(section),
            P(HEAD, rows),
        ),
        out_specs=P(section, KV, HEAD),
        check_vma=False,
    )
```
